32 devices in a mesh: gx: 8 (over z, x), gy: 4 (over y, core).
Axes of the slice: x: 2, y: 2, z: 4, core: 2. Of those that a mesh axis runs over, the one named last changes fastest.
Arguments:
- mean_field: float32 [16, 128, 1024], P(None, 'gx', 'gy'), may hold values from -6 to 6
- mode_fields: float32 [16, 16, 128, 1024], P(None, None, 'gx', 'gy'), may hold values from -6 to 6
- velocity_east: float32 [16, 128, 1024], P(None, 'gx', 'gy'), may hold values from -6 to 6
- velocity_north: float32 [16, 128, 1024], P(None, 'gx', 'gy'), may hold values from -6 to 6
- flag_east: int32 [16, 128, 1024], P(None, 'gx', 'gy'), may hold values 0 or 1
- flag_north: int32 [16, 128, 1024], P(None, 'gx', 'gy'), may hold values 0 or 1
- ocean_mask: int32 [16, 128, 1024], P(None, 'gx', 'gy'), may hold values 0 or 1
Outputs:
- mean_next: float32 [16, 128, 1024], P(None, 'gx', 'gy')
- modes_next: float32 [16, 16, 128, 1024], P(None, None, 'gx', 'gy')
- factor: float32 [16, 16], replicated
The draws below stay inside these ranges and needn't reach their ends.
Inputs may be any that keep to these rules, and one draw needn't show every extreme that they name: `flag_east`: 1 takes the five-point upwind value biased to the cell of lower index beside the face, 0 the one biased to the higher. `flag_north`: as for the first dimension. `ocean_mask`: 1 marks ocean, 0 land.
All inputs are finite; a program needn't handle non-finite values. No bound on the sum of `flag_east` or of `flag_north` or of `ocean_mask` on one device may be relied on, other than what follows from the above.
Results may differ from the reference program's by a relative error of at most 0.0003.
Values sent between devices are 32-bit elements; how exact they have to be, the bound alone decides.
A program may use at most 128 MiB of HBM per device.

```python
import jax
import jax.numpy as jnp
from jax import lax

M = 16
NZ = 16
NX = 128
NY = 1024


def with_ends(values, stream_key, low, high):
    spot = [jax.random.randint(jax.random.fold_in(stream_key, axis), (), 0, length) for axis, length in enumerate(values.shape)]
    main_axis = values.shape.index(max(values.shape))
    next_to = spot[:main_axis] + [(spot[main_axis] + 1) % values.shape[main_axis]] + spot[main_axis + 1:]
    return values.at[tuple(spot)].set(low).at[tuple(next_to)].set(high)


def block_scale(rng, shape, cuts, least, top_value):
    loudness = 1.0
    for position, parts in cuts:
        heights = jax.random.uniform(jax.random.fold_in(jax.random.fold_in(rng, 6), position), (parts,), jnp.float32, least / len(cuts), top_value / len(cuts))
        loudness = loudness * jnp.repeat(jnp.exp(heights), shape[position] // parts).reshape((-1,) + (1,) * (len(shape) - 1 - position))
    return loudness


def scatter_about(rng, dims, width, bound, cuts=(), held_as=jnp.bfloat16):
    result = width * jax.random.normal(rng, dims, jnp.float32)
    if cuts:
        result = result * block_scale(rng, dims, cuts, -0.22, 0.18)
    return jnp.clip(result, -bound, bound).astype(held_as)


def setup_inputs(seed: int = 0) -> dict:
    key_of = jax.random.split(jax.random.key(seed), 8)
    return {
        "mean_field": scatter_about(key_of[0], (NZ, NX, NY), 1.0, 6.0, ((1, 8), (2, 4)), jnp.float32),
        "mode_fields": scatter_about(key_of[1], (M, NZ, NX, NY), 1.0, 6.0, ((2, 8), (3, 4)), jnp.float32),
        "velocity_east": scatter_about(key_of[2], (NZ, NX, NY), 1.0, 6.0, ((1, 8), (2, 4)), jnp.float32),
        "velocity_north": scatter_about(key_of[3], (NZ, NX, NY), 1.0, 6.0, ((1, 8), (2, 4)), jnp.float32),
        "flag_east": with_ends((jax.random.randint(key_of[4], (NZ, NX, NY), 0, 2) < 1).astype(jnp.int32), jax.random.fold_in(key_of[4], 1), 0, 1),
        "flag_north": with_ends((jax.random.randint(key_of[5], (NZ, NX, NY), 0, 2) < 1).astype(jnp.int32), jax.random.fold_in(key_of[5], 1), 0, 1),
        "ocean_mask": with_ends((jax.random.randint(key_of[6], (NZ, NX, NY), 0, 10) < 9).astype(jnp.int32), jax.random.fold_in(key_of[6], 1), 0, 1),
    }


time_step = 0.1
horiz_diff = 0.05
vert_diff = 0.2

def cells_at(values, axis_dim, first_face, face_count, offset):
    start_index = first_face + offset + 3
    return lax.slice_in_dim(values, start_index, start_index + face_count, axis=axis_dim)

def face_fluxes(values, openness, pos_speed, neg_speed, axis_dim, first_face, face_count):
    centre = cells_at(values, axis_dim, first_face, face_count, 0)
    upper_one = cells_at(values, axis_dim, first_face, face_count, 1)
    lower_one = cells_at(values, axis_dim, first_face, face_count, -1)
    upper_two = cells_at(values, axis_dim, first_face, face_count, 2)
    left_side = (2.0 * cells_at(values, axis_dim, first_face, face_count, -2) - 13.0 * lower_one + 47.0 * centre + 27.0 * upper_one - 3.0 * upper_two) / 60.0
    right_side = (2.0 * cells_at(values, axis_dim, first_face, face_count, 3) - 13.0 * upper_two + 47.0 * upper_one + 27.0 * centre - 3.0 * lower_one) / 60.0
    return openness * (pos_speed * left_side + neg_speed * right_side - horiz_diff * (upper_one - centre))

def direction_fluxes(channels, pos_speed, neg_speed, axis_dim, first_face, face_count):
    mask_part = channels[-1]
    field_part = channels[:-1]
    openness = cells_at(mask_part, axis_dim - 1, first_face, face_count, 0) * cells_at(mask_part, axis_dim - 1, first_face, face_count, 1)
    return face_fluxes(field_part, openness, pos_speed, neg_speed, axis_dim, first_face, face_count)

def lower_inverse(lower_factor):
    order_size = lower_factor.shape[0]
    identity = jnp.eye(order_size, dtype=lower_factor.dtype)
    rows_out = []
    for row_index in range(order_size):
        partial_value = identity[row_index]
        for col_index in range(row_index):
            partial_value = partial_value - lower_factor[row_index, col_index] * rows_out[col_index]
        rows_out.append(partial_value / lower_factor[row_index, row_index])
    return jnp.stack(rows_out)

def reference(mean_field, mode_fields, velocity_east, velocity_north, flag_east, flag_north, ocean_mask):
    fields = jnp.concatenate([mean_field[None], mode_fields], axis=0)
    wet_cells = ocean_mask.astype(jnp.float32)
    east_flag = flag_east.astype(jnp.float32)
    north_flag = flag_north.astype(jnp.float32)
    pos_east = velocity_east * east_flag
    neg_east = velocity_east * (1.0 - east_flag)
    pos_north = velocity_north * north_flag
    neg_north = velocity_north * (1.0 - north_flag)
    levels = fields.shape[1]
    size_x = fields.shape[2]
    size_y = fields.shape[3]

    def level_tendency(level_index):
        fields_here = lax.dynamic_index_in_dim(fields, level_index, 1, keepdims=False)
        level_above = lax.dynamic_index_in_dim(fields, jnp.minimum(level_index + 1, levels - 1), 1, keepdims=False)
        level_below = lax.dynamic_index_in_dim(fields, jnp.maximum(level_index - 1, 0), 1, keepdims=False)
        planes = [lax.dynamic_index_in_dim(plane, level_index, 0, keepdims=False) for plane in (wet_cells, pos_east, neg_east, pos_north, neg_north)]
        stacked = jnp.concatenate([fields_here] + [plane[None] for plane in planes], axis=0)
        padded = jnp.pad(stacked, ((0, 0), (3, 3), (3, 3)))
        across_x = padded[:, :, 3:-3]
        flux_east = direction_fluxes(across_x[:-4], cells_at(across_x[-4], 0, -1, size_x + 1, 0), cells_at(across_x[-3], 0, -1, size_x + 1, 0), 1, -1, size_x + 1)
        tend_x = flux_east[:, :-1] - flux_east[:, 1:]
        across_y = padded[:, 3:-3, :]
        flux_north = direction_fluxes(across_y[:-4], cells_at(across_y[-2], 1, -1, size_y + 1, 0), cells_at(across_y[-1], 1, -1, size_y + 1, 0), 2, -1, size_y + 1)
        tend_y = flux_north[:, :, :-1] - flux_north[:, :, 1:]
        up_flux = jnp.where(level_index < levels - 1, vert_diff * (level_above - fields_here), 0.0)
        down_flux = jnp.where(level_index > 0, vert_diff * (fields_here - level_below), 0.0)
        return planes[0] * (tend_x + tend_y + (up_flux - down_flux))
    per_level = lax.map(level_tendency, jnp.arange(levels, dtype=jnp.int32))
    tendency = jnp.moveaxis(per_level, 0, 1)
    mean_next = mean_field + time_step * tendency[0]
    mode_count = mode_fields.shape[0]
    flat_modes = mode_fields.reshape(mode_count, -1)
    flat_tend = tendency[1:].reshape(mode_count, -1)
    cell_count = float(flat_modes.shape[1])
    highest = lax.Precision.HIGHEST
    projection = jnp.dot(flat_modes, flat_tend.T, precision=highest) / cell_count
    growth = flat_tend - jnp.dot(projection.T, flat_modes, precision=highest)
    updated = flat_modes + time_step * growth
    gram_matrix = jnp.dot(updated, updated.T, precision=highest) / cell_count
    lower_factor = jnp.linalg.cholesky(gram_matrix)
    inverse = lower_inverse(lower_factor)
    modes_next = jnp.dot(inverse, updated, precision=highest).reshape(mode_fields.shape)
    return (mean_next, modes_next, lower_factor.T)
```

```python
import functools

import jax
import jax.numpy as jnp
from jax import lax
from jax.experimental import pallas as pl
from jax.experimental.pallas import tpu as pltpu
from jax.sharding import PartitionSpec as P

time_step = 0.1
horiz_diff = 0.05
vert_diff = 0.2
HALO = 3
LANES = 128
SUB = 8
AHEAD = 4
HIGHEST = lax.Precision.HIGHEST
MESH = pl.DeviceIdType.MESH
SHIFTS = (-3, -2, -1, 1, 2, 3)


def blocked(array):
    *lead, size_x, size_y = array.shape
    at = len(lead)
    return jnp.swapaxes(array.reshape(*lead, size_x // SUB, SUB, size_y // LANES, LANES), at + 1, at + 2)


def unblocked(array):
    *lead, high, wide, sub, lanes = array.shape
    at = len(lead)
    return jnp.swapaxes(array, at + 1, at + 2).reshape(*lead, high * sub, wide * lanes)


def face_weights(pos, neg, openness):
    return {
        -2: openness * (2.0 * pos) / 60.0,
        -1: openness * (-13.0 * pos - 3.0 * neg) / 60.0,
        0: openness * ((47.0 * pos + 27.0 * neg) / 60.0 + horiz_diff),
        1: openness * ((27.0 * pos + 47.0 * neg) / 60.0 - horiz_diff),
        2: openness * (-3.0 * pos - 13.0 * neg) / 60.0,
        3: openness * (2.0 * neg) / 60.0,
    }


def stencil(speed, side, cells, speed_before, side_before, cells_before, cells_after, axis):
    size = cells.shape[axis]
    spot = lax.broadcasted_iota(jnp.int32, cells.shape, axis)
    beyond = jnp.where(spot == size - 1, cells_after, pltpu.roll(cells, size - 1, axis))
    face = face_weights(speed * side, speed * (1.0 - side), cells * beyond)
    first = cells[:1, :] if axis == 0 else cells[:, :1]
    entry = face_weights(speed_before * side_before, speed_before * (1.0 - side_before), cells_before * first)
    result = {}
    for s in range(-3, 4):
        value = 0.0
        if s + 1 in face:
            value = value + jnp.where(spot == 0, entry[s + 1], pltpu.roll(face[s + 1], 1, axis))
        if s in face:
            value = value - face[s]
        result[s] = cells * value
    return result


def f32(value):
    return value.astype(jnp.float32)


def tend_kernel(
    nx, ny,
    modes_in, mean_in, east_in, north_in, flag_east_in, flag_north_in, mask_in,
    tend_out, mean_out, gram,
    ext, left, right, ext_mean, left_mean, right_mean, relay, tend, mean_next,
    east, north, flag_east, flag_north, mask,
    east_low, flag_low, mask_low, mask_high,
    north_left, flag_left, mask_left, mask_right,
    coefs, total, mine, middle, along_y, along_x,
    load_sem, plane_sem, up_send, down_send, pass_send, low_recv, high_recv, relay_recv,
    right_send, left_send, left_recv, right_recv,
    aux_send, aux_recv, mean_send, mean_recv, out_sem, send_y, recv_y, send_x, recv_x,
):
    count, levels, high, wide, _, _ = modes_in.shape
    size_x, size_y = high * SUB, wide * LANES
    gx, gy = lax.axis_index("gx"), lax.axis_index("gy")
    half = nx // 2
    odd = lax.rem(gx, 2)
    pair = lax.div(gx, 2)
    has_up, has_down = gx < nx - 1, gx > 0
    has_right, has_left = gy < ny - 1, gy > 0
    up, down = jnp.minimum(gx + 1, nx - 1), jnp.maximum(gx - 1, 0)
    up_two, down_two = jnp.minimum(gx + 2, nx - 1), jnp.maximum(gx - 2, 0)
    to_right, to_left = jnp.minimum(gy + 1, ny - 1), jnp.maximum(gy - 1, 0)
    up_turns = jnp.where((odd == 1) & has_up, pair + 1, 0)
    down_turns = jnp.where((odd == 0) & has_down, half - pair, 0)
    pass_down_turns = jnp.where(odd == 1, pair, 0)
    pass_up_turns = jnp.where(odd == 0, half - 1 - pair, 0)
    barrier = pltpu.get_barrier_semaphore()

    def next_y(k):
        return lax.rem(gy + k, ny)

    def next_x(k):
        return lax.rem(gx + k, nx)

    for k in range(1, ny):
        pl.semaphore_signal(barrier, inc=1, device_id=(gx, next_y(k)), device_id_type=MESH)
    for k in range(1, nx):
        pl.semaphore_signal(barrier, inc=1, device_id=(next_x(k), gy), device_id_type=MESH)

    def remote(src, dst, send, recv, x, y):
        return pltpu.make_async_remote_copy(
            src_ref=src, dst_ref=dst, send_sem=send, recv_sem=recv, device_id=(x, y), device_id_type=MESH
        )

    def load_level(k):
        return [
            pltpu.make_async_copy(
                modes_in.at[:, k, h], ext.at[:, k, :, pl.ds(SUB + SUB * h, SUB), :], load_sem.at[k, h]
            )
            for h in range(high)
        ]

    plane_loads = [
        pltpu.make_async_copy(src, dst, plane_sem.at[i])
        for i, (src, dst) in enumerate(
            [(east_in, east), (flag_east_in, flag_east), (mask_in, mask), (north_in, north), (flag_north_in, flag_north)]
        )
    ] + [
        pltpu.make_async_copy(mean_in.at[:, h], ext_mean.at[0, :, :, pl.ds(SUB + SUB * h, SUB), :], plane_sem.at[5 + h])
        for h in range(high)
    ]

    last, first = pl.ds(SUB - HALO, HALO), pl.ds(0, HALO)
    end = pl.ds(SUB + size_x, HALO)
    last_row = pl.ds(SUB - 1, 1)
    first_row = pl.ds(0, 1)

    aux_up = [
        remote(src.at[:, high - 1, :, last_row, :], dst.at[:, :, last_row, :], aux_send.at[i], aux_recv.at[i], up, gy)
        for i, (src, dst) in enumerate([(east_in, east_low), (flag_east_in, flag_low), (mask_in, mask_low)])
    ]
    aux_down = [
        remote(mask_in.at[:, 0, :, first_row, :], mask_high.at[:, :, first_row, :], aux_send.at[3], aux_recv.at[3], down, gy)
    ]
    aux_right = [
        remote(src.at[:, :, wide - 1], dst, aux_send.at[4 + i], aux_recv.at[4 + i], gx, to_right)
        for i, (src, dst) in enumerate([(north_in, north_left), (flag_north_in, flag_left), (mask_in, mask_left)])
    ]
    aux_left = [remote(mask_in.at[:, :, 0], mask_right, aux_send.at[7], aux_recv.at[7], gx, to_left)]

    def up_copy(k):
        return remote(
            modes_in.at[:, k, high - 1, :, last, :], ext.at[:, k, :, last, :], up_send.at[k], low_recv.at[k], up, gy
        )

    def up_relay(k):
        return remote(
            modes_in.at[:, k, high - 1, :, last, :], relay.at[k, :, :, first, :], up_send.at[k], relay_recv.at[k], up_two, gy
        )

    def down_copy(k):
        return remote(
            modes_in.at[:, k, 0, :, first, :], ext.at[:, k, :, end, :], down_send.at[k], high_recv.at[k], down, gy
        )

    def down_relay(k):
        return remote(
            modes_in.at[:, k, 0, :, first, :], relay.at[k, :, :, first, :], down_send.at[k], relay_recv.at[k], down_two, gy
        )

    def pass_down(k):
        return remote(relay.at[k, :, :, first, :], ext.at[:, k, :, last, :], pass_send.at[k], low_recv.at[k], down, gy)

    def pass_up(k):
        return remote(relay.at[k, :, :, first, :], ext.at[:, k, :, end, :], pass_send.at[k], high_recv.at[k], up, gy)

    def right_copy(k):
        return remote(modes_in.at[:, k, :, wide - 1], left.at[:, k], right_send.at[k], left_recv.at[k], gx, to_right)

    def left_copy(k):
        return remote(modes_in.at[:, k, :, 0], right.at[:, k], left_send.at[k], right_recv.at[k], gx, to_left)

    mean_up = remote(
        mean_in.at[:, high - 1, :, last, :], ext_mean.at[0, :, :, last, :], mean_send.at[0], mean_recv.at[0], up, gy
    )
    mean_down = remote(
        mean_in.at[:, 0, :, first, :], ext_mean.at[0, :, :, end, :], mean_send.at[1], mean_recv.at[1], down, gy
    )
    mean_right = remote(mean_in.at[:, :, wide - 1], left_mean.at[0], mean_send.at[2], mean_recv.at[2], gx, to_right)
    mean_left = remote(mean_in.at[:, :, 0], right_mean.at[0], mean_send.at[3], mean_recv.at[3], gx, to_left)

    def turn(k):
        return lax.rem(k, half)

    def send_x_level(k):
        @pl.when(has_up & (turn(k) >= up_turns))
        def _():
            up_copy(k).start()

        @pl.when(has_down & (turn(k) >= down_turns))
        def _():
            down_copy(k).start()

    def pass_level(k):
        @pl.when(turn(k) < pass_down_turns)
        def _():
            up_relay(k).wait_recv()
            pass_down(k).start()

        @pl.when(turn(k) < pass_up_turns)
        def _():
            down_relay(k).wait_recv()
            pass_up(k).start()

    for k in range(levels):
        for copy in load_level(k):
            copy.start()
        if k == 0:
            for copy in plane_loads:
                copy.start()

    def zero_low(k, carry):
        for t in range(wide):
            ext[:, k, t, :SUB, :] = jnp.zeros((count, SUB, LANES), jnp.float32)
            ext_mean[:, k, t, :SUB, :] = jnp.zeros((1, SUB, LANES), jnp.float32)
        return carry

    def zero_high(k, carry):
        for t in range(wide):
            ext[:, k, t, SUB + size_x :, :] = jnp.zeros((count, SUB, LANES), jnp.float32)
            ext_mean[:, k, t, SUB + size_x :, :] = jnp.zeros((1, SUB, LANES), jnp.float32)
        return carry

    def zero_left(k, carry):
        left[:, k] = jnp.zeros((count, high, SUB, LANES), jnp.float32)
        left_mean[:, k] = jnp.zeros((1, high, SUB, LANES), jnp.float32)
        return carry

    def zero_right(k, carry):
        right[:, k] = jnp.zeros((count, high, SUB, LANES), jnp.float32)
        right_mean[:, k] = jnp.zeros((1, high, SUB, LANES), jnp.float32)
        return carry

    @pl.when(~has_down)
    def _():
        lax.fori_loop(0, levels, zero_low, 0)
        for ref in (east_low, flag_low, mask_low):
            ref[...] = jnp.zeros_like(ref)

    @pl.when(~has_up)
    def _():
        lax.fori_loop(0, levels, zero_high, 0)
        mask_high[...] = jnp.zeros_like(mask_high)

    @pl.when(~has_left)
    def _():
        lax.fori_loop(0, levels, zero_left, 0)
        for ref in (north_left, flag_left, mask_left):
            ref[...] = jnp.zeros_like(ref)

    @pl.when(~has_right)
    def _():
        lax.fori_loop(0, levels, zero_right, 0)
        mask_right[...] = jnp.zeros_like(mask_right)

    total[...] = jnp.zeros_like(total)

    pl.semaphore_wait(barrier, nx + ny - 2)

    @pl.when(has_up)
    def _():
        for copy in aux_up:
            copy.start()

    @pl.when(has_down)
    def _():
        for copy in aux_down:
            copy.start()

    for k in range(min(AHEAD, levels)):
        send_x_level(k)

    def send_relayed(k, carry):
        @pl.when(turn(k) < up_turns)
        def _():
            up_relay(k).start()

        @pl.when(turn(k) < down_turns)
        def _():
            down_relay(k).start()

        return carry

    lax.fori_loop(0, levels, send_relayed, 0)

    @pl.when(has_right)
    def _():
        for copy in aux_right:
            copy.start()

    @pl.when(has_left)
    def _():
        for copy in aux_left:
            copy.start()

    def send_y_level(k, carry):
        @pl.when(has_right)
        def _():
            right_copy(k).start()

        @pl.when(has_left)
        def _():
            left_copy(k).start()

        return carry

    lax.fori_loop(0, levels, send_y_level, 0)

    for copy in plane_loads:
        copy.wait()

    def wait_loaded(k, carry):
        for copy in load_level(k):
            copy.wait()
        return carry

    lax.fori_loop(0, levels, wait_loaded, 0)

    for k in range(min(AHEAD, levels)):
        pass_level(k)

    @pl.when(has_down)
    def _():
        for copy in aux_up:
            copy.wait_recv()

    @pl.when(has_up)
    def _():
        for copy in aux_down:
            copy.wait_recv()

    @pl.when(has_left)
    def _():
        for copy in aux_right:
            copy.wait_recv()

    @pl.when(has_right)
    def _():
        for copy in aux_left:
            copy.wait_recv()

    lane = lax.broadcasted_iota(jnp.int32, (SUB, LANES), 1)

    def plane(ref, k):
        return jnp.concatenate(
            [jnp.concatenate([f32(ref[k, h, t]) for t in range(wide)], axis=1) for h in range(high)], axis=0
        )

    def edge_row(ref, k, row):
        return jnp.concatenate([f32(ref[k, t, row : row + 1, :]) for t in range(wide)], axis=1)

    def edge_column(ref, k, column):
        return jnp.concatenate([f32(ref[k, h])[:, column : column + 1] for h in range(high)], axis=0)

    def level_coefs(k):
        wet = plane(mask, k)
        dx = stencil(
            plane(east, k), plane(flag_east, k), wet,
            edge_row(east_low, k, SUB - 1), edge_row(flag_low, k, SUB - 1), edge_row(mask_low, k, SUB - 1),
            edge_row(mask_high, k, 0), 0,
        )
        dy = stencil(
            plane(north, k), plane(flag_north, k), wet,
            edge_column(north_left, k, LANES - 1), edge_column(flag_left, k, LANES - 1),
            edge_column(mask_left, k, LANES - 1), edge_column(mask_right, k, 0), 1,
        )
        upright = vert_diff * wet
        return [dx[s] for s in SHIFTS] + [dy[s] for s in SHIFTS] + [dx[0] + dy[0] - 2.0 * upright, upright]

    def moved(row, s):
        if s < 0:
            mixed = jnp.where(lane >= LANES + s, row[0], row[1])
        else:
            mixed = jnp.where(lane < s, row[2], row[1])
        return pltpu.roll(mixed, (-s) % LANES, 1)

    def tendency(weights, f, k, h, t, cells, beside_left, beside_right):
        above = jnp.minimum(k + 1, levels - 1)
        below = jnp.maximum(k - 1, 0)
        base = SUB + SUB * h
        cut = slice(base, base + SUB)
        c = cells[f, k, t, cut, :]
        before = cells[f, k, t - 1, cut, :] if t > 0 else beside_left[f, k, h]
        after = cells[f, k, t + 1, cut, :] if t < wide - 1 else beside_right[f, k, h]
        row = [before, c, after]
        value = weights[12] * c + weights[13] * (cells[f, above, t, cut, :] + cells[f, below, t, cut, :])
        for i, s in enumerate(SHIFTS):
            value += weights[i] * cells[f, k, t, base + s : base + s + SUB, :]
            value += weights[6 + i] * moved(row, s)
        return value

    def store_tend(k):
        return pltpu.make_async_copy(tend.at[k], tend_out.at[k], out_sem.at[k])

    contract = (((1,), (1,)), ((), ()))

    def split(values):
        coarse = values.astype(jnp.bfloat16)
        return coarse, (values - f32(coarse)).astype(jnp.bfloat16)

    def level(k, carry):
        @pl.when(k + AHEAD < levels)
        def _():
            send_x_level(k + AHEAD)
            pass_level(k + AHEAD)

        @pl.when(k + AHEAD == levels)
        def _():
            @pl.when(has_up)
            def _():
                mean_up.start()

            @pl.when(has_down)
            def _():
                mean_down.start()

            @pl.when(has_right)
            def _():
                mean_right.start()

            @pl.when(has_left)
            def _():
                mean_left.start()

        for i, value in enumerate(level_coefs(k)):
            coefs[k, i] = value

        @pl.when(has_left)
        def _():
            right_copy(k).wait_recv()

        @pl.when(has_right)
        def _():
            left_copy(k).wait_recv()

        @pl.when(has_down)
        def _():
            up_copy(k).wait_recv()

        @pl.when(has_up)
        def _():
            down_copy(k).wait_recv()

        for h in range(high):
            for t in range(wide):
                weights = [
                    coefs[k, i, SUB * h : SUB * (h + 1), LANES * t : LANES * (t + 1)] for i in range(len(SHIFTS) * 2 + 2)
                ]
                for f in range(count):
                    tend[k, h * wide + t, SUB * f : SUB * (f + 1), :] = tendency(
                        weights, f, k, h, t, ext, left, right
                    )
        store_tend(k).start()
        u = jnp.concatenate(
            [
                ext[:, k, t, SUB + SUB * h : SUB + SUB * (h + 1), :].reshape(count * SUB, LANES)
                for h in range(high)
                for t in range(wide)
            ],
            axis=1,
        )
        v = jnp.concatenate([tend[k, i] for i in range(high * wide)], axis=1)
        coarse, fine = split(jnp.concatenate([u, v], axis=0))
        total[...] += lax.dot_general(
            jnp.concatenate([coarse, fine], axis=0), coarse, contract, preferred_element_type=jnp.float32
        )
        return carry

    lax.fori_loop(0, levels, level, 0)

    def copy_y(k, slot):
        return remote(mine, along_y.at[slot], send_y.at[k], recv_y.at[slot], gx, next_y(k))

    def copy_x(k, slot):
        return remote(middle, along_x.at[slot], send_x.at[k], recv_x.at[slot], next_x(k), gy)

    tall = 2 * count * SUB
    row = lax.broadcasted_iota(jnp.int32, (tall, tall), 0)
    col = lax.broadcasted_iota(jnp.int32, (tall, tall), 1)
    cross = total[tall:, :]
    summed = jnp.where((row % SUB) == (col % SUB), total[:tall, :] + cross + cross.T, 0.0)
    pick = f32(
        lax.broadcasted_iota(jnp.int32, (2 * count, tall), 1) // SUB
        == lax.broadcasted_iota(jnp.int32, (2 * count, tall), 0)
    )
    height, width = gram.shape
    spread = f32(
        lax.broadcasted_iota(jnp.int32, (tall, width), 0) // SUB
        == lax.broadcasted_iota(jnp.int32, (tall, width), 1) % (2 * count)
    )
    part = jnp.dot(pick, summed, precision=HIGHEST, preferred_element_type=jnp.float32)
    full = jnp.dot(part, spread, precision=HIGHEST, preferred_element_type=jnp.float32)
    block = lax.broadcasted_iota(jnp.int32, gram.shape, 1) // (2 * count)
    packed = full[:height]
    for b in range(1, 2 * count // height):
        packed = jnp.where(block == b, full[b * height : (b + 1) * height], packed)
    mine[...] = packed
    along_y[gy] = packed
    for k in range(1, ny):
        copy_y(k, gy).start()
    for k in range(1, ny):
        copy_y(k, next_y(k)).wait_recv()
    summed = along_y[0]
    for k in range(1, ny):
        summed = summed + along_y[k]
    middle[...] = summed
    along_x[gx] = summed
    for k in range(1, nx):
        copy_x(k, gx).start()

    @pl.when(has_down)
    def _():
        mean_up.wait_recv()

    @pl.when(has_up)
    def _():
        mean_down.wait_recv()

    @pl.when(has_left)
    def _():
        mean_right.wait_recv()

    @pl.when(has_right)
    def _():
        mean_left.wait_recv()

    def mean_level(k, carry):
        for h in range(high):
            for t in range(wide):
                weights = [
                    coefs[k, i, SUB * h : SUB * (h + 1), LANES * t : LANES * (t + 1)] for i in range(len(SHIFTS) * 2 + 2)
                ]
                value = tendency(weights, 0, k, h, t, ext_mean, left_mean, right_mean)
                mean_next[k, h, t] = ext_mean[0, k, t, SUB + SUB * h : SUB + SUB * (h + 1), :] + time_step * value
        return carry

    lax.fori_loop(0, levels, mean_level, 0)
    store_mean = pltpu.make_async_copy(mean_next, mean_out, plane_sem.at[0])
    store_mean.start()

    for k in range(1, nx):
        copy_x(k, next_x(k)).wait_recv()
    summed = along_x[0]
    for k in range(1, nx):
        summed = summed + along_x[k]
    gram[...] = summed

    for k in range(1, ny):
        copy_y(k, gy).wait_send()
    for k in range(1, nx):
        copy_x(k, gx).wait_send()

    def settle(k, carry):
        @pl.when(has_up)
        def _():
            up_copy(k).wait_send()

        @pl.when(has_down)
        def _():
            down_copy(k).wait_send()

        @pl.when((turn(k) < pass_down_turns) | (turn(k) < pass_up_turns))
        def _():
            pass_down(k).wait_send()

        @pl.when(has_right)
        def _():
            right_copy(k).wait_send()

        @pl.when(has_left)
        def _():
            left_copy(k).wait_send()

        store_tend(k).wait()
        return carry

    lax.fori_loop(0, levels, settle, 0)
    for there, copies in (
        (has_up, aux_up + [mean_up]),
        (has_down, aux_down + [mean_down]),
        (has_right, aux_right + [mean_right]),
        (has_left, aux_left + [mean_left]),
    ):

        @pl.when(there)
        def _():
            for copy in copies:
                copy.wait_send()

    store_mean.wait()


def solve(packed, count, cells):
    two = 2 * count
    height, width = packed.shape
    block = lax.broadcasted_iota(jnp.int32, packed.shape, 1) // two
    stacked = jnp.concatenate([jnp.where(block == b, packed, 0.0) for b in range(two // height)], axis=0)
    fold = (
        lax.broadcasted_iota(jnp.int32, (width, two), 0) % two == lax.broadcasted_iota(jnp.int32, (width, two), 1)
    ).astype(jnp.float32)
    total = jnp.dot(stacked, fold, precision=HIGHEST, preferred_element_type=jnp.float32) / cells
    row = lax.broadcasted_iota(jnp.int32, (count, two), 0)
    col = lax.broadcasted_iota(jnp.int32, (count, two), 1)
    contract = (((1,), (1,)), ((), ()))
    update = jnp.where(
        col < count,
        jnp.where(col == row, 1.0, 0.0) - time_step * total[count:, :],
        jnp.where(col == row + count, time_step, 0.0),
    )
    padding = jnp.zeros((count, two), jnp.float32)
    halfway = jnp.dot(update, total, precision=HIGHEST, preferred_element_type=jnp.float32)
    work = lax.dot_general(
        halfway,
        jnp.concatenate([update, padding], axis=0),
        contract,
        precision=HIGHEST,
        preferred_element_type=jnp.float32,
    )
    work = work + jnp.where(col == row + count, 1.0, 0.0)
    for j in range(count):
        column = jnp.broadcast_to(work[:, j : j + 1], (count, two))
        scale = lax.rsqrt(column[j : j + 1, :])
        pivot_row = work[j : j + 1, :] * scale
        work = jnp.where(row > j, work - (column * scale) * pivot_row, jnp.where(row == j, pivot_row, work))
    factor = jnp.where(col >= row, work, 0.0)[:, :count]
    inverse = jnp.where(col >= count, work, 0.0)
    mix = jnp.dot(
        inverse,
        jnp.concatenate([padding, update], axis=0),
        precision=HIGHEST,
        preferred_element_type=jnp.float32,
    )
    return factor, mix


def combine_kernel(
    cells, packed, modes_in, tend_in, mean_in, out, mean_out, factor,
    modes, tend, mean, result, weights, modes_sem, tend_sem, mean_sem, out_sem,
):
    count, levels, high, wide, _, _ = modes_in.shape
    tall, both_tall = count * SUB, 2 * count * SUB

    def load(k):
        return [
            pltpu.make_async_copy(modes_in.at[:, k], modes.at[:, k], modes_sem.at[k]),
            pltpu.make_async_copy(tend_in.at[k], tend.at[k], tend_sem.at[k]),
        ]

    def store(k):
        return pltpu.make_async_copy(result.at[:, k], out.at[:, k], out_sem.at[k])

    for k in range(levels):
        for copy in load(k):
            copy.start()
    load_mean = pltpu.make_async_copy(mean_in, mean, mean_sem.at[0])
    load_mean.start()

    factor[...], mix = solve(packed[...], count, cells)
    spread = (
        lax.broadcasted_iota(jnp.int32, (tall, count), 0) // SUB == lax.broadcasted_iota(jnp.int32, (tall, count), 1)
    ).astype(jnp.float32)
    along = (
        lax.broadcasted_iota(jnp.int32, (2 * count, both_tall), 1) // SUB
        == lax.broadcasted_iota(jnp.int32, (2 * count, both_tall), 0)
    ).astype(jnp.float32)
    whole = jnp.dot(
        jnp.dot(spread, mix, precision=HIGHEST, preferred_element_type=jnp.float32),
        along,
        precision=HIGHEST,
        preferred_element_type=jnp.float32,
    )
    row = lax.broadcasted_iota(jnp.int32, (tall, both_tall), 0)
    col = lax.broadcasted_iota(jnp.int32, (tall, both_tall), 1)
    whole = jnp.where((row % SUB) == (col % SUB), whole, 0.0)
    coarse = whole.astype(jnp.bfloat16)
    weights[:tall, :] = coarse
    weights[tall:, :] = (whole - coarse.astype(jnp.float32)).astype(jnp.bfloat16)
    load_mean.wait()
    store_mean = pltpu.make_async_copy(mean, mean_out, mean_sem.at[1])
    store_mean.start()

    def level(k, carry):
        for copy in load(k):
            copy.wait()
        both = jnp.concatenate(
            [
                jnp.concatenate(
                    [modes[:, k, h, t].reshape(tall, LANES), tend[k, h * wide + t]], axis=0
                )
                for h in range(high)
                for t in range(wide)
            ],
            axis=1,
        )
        coarse = both.astype(jnp.bfloat16)
        fine = (both - coarse.astype(jnp.float32)).astype(jnp.bfloat16)
        main = jnp.dot(weights[...], coarse, preferred_element_type=jnp.float32)
        mixed = main[:tall] + (main[tall:] + jnp.dot(weights[:tall, :], fine, preferred_element_type=jnp.float32))
        for h in range(high):
            for t in range(wide):
                i = h * wide + t
                result[:, k, h, t] = mixed[:, LANES * i : LANES * (i + 1)].reshape(count, SUB, LANES)
        store(k).start()
        return carry

    lax.fori_loop(0, levels, level, 0)

    def settle(k, carry):
        store(k).wait()
        return carry

    lax.fori_loop(0, levels, settle, 0)
    store_mean.wait()


def section(mean_field, mode_fields, velocity_east, velocity_north, flag_east, flag_north, ocean_mask):
    count, levels, size_x, size_y = mode_fields.shape
    nx, ny = lax.axis_size("gx"), lax.axis_size("gy")
    high, wide = size_x // SUB, size_y // LANES
    real, whole = jnp.float32, jnp.int32
    anywhere = pl.BlockSpec(memory_space=pl.ANY)
    vmem = pl.BlockSpec(memory_space=pltpu.VMEM)
    modes = blocked(mode_fields)
    planes = [blocked(a) for a in (mean_field, velocity_east, velocity_north, flag_east, flag_north, ocean_mask)]
    plane = (levels, high, wide, SUB, LANES)
    tall = 2 * count * SUB
    packed = (4 * count * count // LANES, LANES)
    spots = len(SHIFTS) * 2 + 2
    dma = pltpu.SemaphoreType.DMA
    edge_row, edge_side = (levels, wide, SUB, LANES), (levels, high, SUB, LANES)
    tend, mean_next, gram = pl.pallas_call(
        functools.partial(tend_kernel, nx, ny),
        in_specs=[anywhere] * 7,
        out_specs=[anywhere, anywhere, vmem],
        out_shape=[
            jax.ShapeDtypeStruct((levels, high * wide, count * SUB, LANES), real),
            jax.ShapeDtypeStruct(plane, real),
            jax.ShapeDtypeStruct(packed, real),
        ],
        scratch_shapes=[
            pltpu.VMEM((count, levels, wide, size_x + 2 * SUB, LANES), real),
            pltpu.VMEM((count, levels, high, SUB, LANES), real),
            pltpu.VMEM((count, levels, high, SUB, LANES), real),
            pltpu.VMEM((1, levels, wide, size_x + 2 * SUB, LANES), real),
            pltpu.VMEM((1, levels, high, SUB, LANES), real),
            pltpu.VMEM((1, levels, high, SUB, LANES), real),
            pltpu.VMEM((levels, count, wide, SUB, LANES), real),
            pltpu.VMEM((levels, high * wide, count * SUB, LANES), real),
            pltpu.VMEM(plane, real),
            pltpu.VMEM(plane, real),
            pltpu.VMEM(plane, real),
            pltpu.VMEM(plane, whole),
            pltpu.VMEM(plane, whole),
            pltpu.VMEM(plane, whole),
            pltpu.VMEM(edge_row, real),
            pltpu.VMEM(edge_row, whole),
            pltpu.VMEM(edge_row, whole),
            pltpu.VMEM(edge_row, whole),
            pltpu.VMEM(edge_side, real),
            pltpu.VMEM(edge_side, whole),
            pltpu.VMEM(edge_side, whole),
            pltpu.VMEM(edge_side, whole),
            pltpu.VMEM((levels, spots, size_x, size_y), real),
            pltpu.VMEM((2 * tall, tall), real),
            pltpu.VMEM(packed, real),
            pltpu.VMEM(packed, real),
            pltpu.VMEM((ny,) + packed, real),
            pltpu.VMEM((nx,) + packed, real),
            dma((levels, high)),
            dma((5 + high,)),
        ]
        + [dma((levels,))] * 10
        + [dma((8,)), dma((8,)), dma((4,)), dma((4,)), dma((levels,)), dma((ny,)), dma((ny,)), dma((nx,)), dma((nx,))],
        compiler_params=pltpu.CompilerParams(collective_id=0, has_side_effects=True),
        cost_estimate=pl.CostEstimate(flops=60 * mode_fields.size, bytes_accessed=12 * mode_fields.size, transcendentals=0),
    )(modes, *planes)

    cell_count = float(levels * size_x * size_y * nx * ny)
    modes_next, mean_next, factor = pl.pallas_call(
        functools.partial(combine_kernel, cell_count),
        in_specs=[vmem, anywhere, anywhere, anywhere],
        out_specs=[anywhere, anywhere, vmem],
        out_shape=[
            jax.ShapeDtypeStruct(modes.shape, real),
            jax.ShapeDtypeStruct(plane, real),
            jax.ShapeDtypeStruct((count, count), real),
        ],
        scratch_shapes=[
            pltpu.VMEM(modes.shape, real),
            pltpu.VMEM((levels, high * wide, count * SUB, LANES), real),
            pltpu.VMEM(plane, real),
            pltpu.VMEM(modes.shape, real),
            pltpu.VMEM((tall, tall), jnp.bfloat16),
            dma((levels,)),
            dma((levels,)),
            dma((2,)),
            dma((levels,)),
        ],
    )(gram, modes, tend, mean_next)
    return unblocked(mean_next), unblocked(modes_next), factor


def solution(mesh):
    grid = P(None, "gx", "gy")
    modes = P(None, None, "gx", "gy")
    return jax.shard_map(
        section,
        mesh=mesh,
        in_specs=(grid, modes, grid, grid, grid, grid, grid),
        out_specs=(grid, modes, P()),
        check_vma=False,
    )
```

```python
import functools

import jax
import jax.numpy as jnp
from jax import lax
from jax.experimental import pallas as pl
from jax.experimental.pallas import tpu as pltpu
from jax.sharding import PartitionSpec as P

time_step = 0.1
horiz_diff = 0.05
vert_diff = 0.2
HALO = 3
LANES = 128
SUB = 8
AHEAD = 4
HIGHEST = lax.Precision.HIGHEST
MESH = pl.DeviceIdType.MESH
SHIFTS = (-3, -2, -1, 1, 2, 3)


def blocked(array):
    *lead, size_x, size_y = array.shape
    at = len(lead)
    return jnp.swapaxes(array.reshape(*lead, size_x // SUB, SUB, size_y // LANES, LANES), at + 1, at + 2)


def unblocked(array):
    *lead, high, wide, sub, lanes = array.shape
    at = len(lead)
    return jnp.swapaxes(array, at + 1, at + 2).reshape(*lead, high * sub, wide * lanes)


def face_weights(pos, neg, openness):
    return {
        -2: openness * (2.0 * pos) / 60.0,
        -1: openness * (-13.0 * pos - 3.0 * neg) / 60.0,
        0: openness * ((47.0 * pos + 27.0 * neg) / 60.0 + horiz_diff),
        1: openness * ((27.0 * pos + 47.0 * neg) / 60.0 - horiz_diff),
        2: openness * (-3.0 * pos - 13.0 * neg) / 60.0,
        3: openness * (2.0 * neg) / 60.0,
    }


def stencil(speed, side, cells, speed_before, side_before, cells_before, cells_after, axis):
    size = cells.shape[axis]
    spot = lax.broadcasted_iota(jnp.int32, cells.shape, axis)
    beyond = jnp.where(spot == size - 1, cells_after, pltpu.roll(cells, size - 1, axis))
    face = face_weights(speed * side, speed * (1.0 - side), cells * beyond)
    first = cells[:1, :] if axis == 0 else cells[:, :1]
    entry = face_weights(speed_before * side_before, speed_before * (1.0 - side_before), cells_before * first)
    result = {}
    for s in range(-3, 4):
        value = 0.0
        if s + 1 in face:
            value = value + jnp.where(spot == 0, entry[s + 1], pltpu.roll(face[s + 1], 1, axis))
        if s in face:
            value = value - face[s]
        result[s] = cells * value
    return result


def f32(value):
    return value.astype(jnp.float32)


def tend_kernel(
    nx, ny,
    modes_in, mean_in, east_in, north_in, flag_east_in, flag_north_in, mask_in,
    ext, tend, mean_next, gram,
    left, right, ext_mean, left_mean, right_mean, relay,
    east, north, flag_east, flag_north, mask,
    east_low, flag_low, mask_low, mask_high,
    north_left, flag_left, mask_left, mask_right,
    coefs, total, mine, middle, along_y, along_x,
    load_sem, plane_sem, up_send, down_send, pass_send, low_recv, high_recv, relay_recv,
    right_send, left_send, left_recv, right_recv,
    aux_send, aux_recv, mean_send, mean_recv, chain, send_y, recv_y, send_x, recv_x,
):
    count, levels, high, wide, _, _ = modes_in.shape
    size_x, size_y = high * SUB, wide * LANES
    gx, gy = lax.axis_index("gx"), lax.axis_index("gy")
    half = nx // 2
    odd = lax.rem(gx, 2)
    pair = lax.div(gx, 2)
    has_up, has_down = gx < nx - 1, gx > 0
    has_right, has_left = gy < ny - 1, gy > 0
    up, down = jnp.minimum(gx + 1, nx - 1), jnp.maximum(gx - 1, 0)
    up_two, down_two = jnp.minimum(gx + 2, nx - 1), jnp.maximum(gx - 2, 0)
    to_right, to_left = jnp.minimum(gy + 1, ny - 1), jnp.maximum(gy - 1, 0)
    up_turns = jnp.where(odd == 1, half - 1 - pair, 0)
    down_turns = jnp.where(odd == 0, pair, 0)
    pass_down_turns = jnp.where(odd == 1, pair, 0)
    pass_up_turns = jnp.where(odd == 0, half - 1 - pair, 0)
    barrier = pltpu.get_barrier_semaphore()

    def next_y(k):
        return lax.rem(gy + k, ny)

    def next_x(k):
        return lax.rem(gx + k, nx)

    beside = (
        (has_up, up, gy),
        (has_down, down, gy),
        (gx < nx - 2, up_two, gy),
        (gx > 1, down_two, gy),
        (has_right, gx, to_right),
        (has_left, gx, to_left),
    )
    for there, x, y in beside:

        @pl.when(there)
        def _():
            pl.semaphore_signal(barrier, inc=1, device_id=(x, y), device_id_type=MESH)

    def remote(src, dst, send, recv, x, y):
        return pltpu.make_async_remote_copy(
            src_ref=src, dst_ref=dst, send_sem=send, recv_sem=recv, device_id=(x, y), device_id_type=MESH
        )

    def load_level(k):
        return [
            pltpu.make_async_copy(
                modes_in.at[:, k, h], ext.at[:, k, :, pl.ds(SUB + SUB * h, SUB), :], load_sem.at[k, h]
            )
            for h in range(high)
        ]

    plane_loads = [
        pltpu.make_async_copy(src, dst, plane_sem.at[i])
        for i, (src, dst) in enumerate(
            [(east_in, east), (flag_east_in, flag_east), (mask_in, mask), (north_in, north), (flag_north_in, flag_north)]
        )
    ] + [
        pltpu.make_async_copy(mean_in.at[:, h], ext_mean.at[0, :, :, pl.ds(SUB + SUB * h, SUB), :], plane_sem.at[5 + h])
        for h in range(high)
    ]

    last, first = pl.ds(SUB - HALO, HALO), pl.ds(0, HALO)
    end = pl.ds(SUB + size_x, HALO)
    last_row = pl.ds(SUB - 1, 1)
    first_row = pl.ds(0, 1)

    aux_up = [
        remote(src.at[:, high - 1, :, last_row, :], dst.at[:, :, last_row, :], aux_send.at[i], aux_recv.at[i], up, gy)
        for i, (src, dst) in enumerate([(east_in, east_low), (flag_east_in, flag_low), (mask_in, mask_low)])
    ]
    aux_down = [
        remote(mask_in.at[:, 0, :, first_row, :], mask_high.at[:, :, first_row, :], aux_send.at[3], aux_recv.at[3], down, gy)
    ]
    aux_right = [
        remote(src.at[:, :, wide - 1], dst, aux_send.at[4 + i], aux_recv.at[4 + i], gx, to_right)
        for i, (src, dst) in enumerate([(north_in, north_left), (flag_north_in, flag_left), (mask_in, mask_left)])
    ]
    aux_left = [remote(mask_in.at[:, :, 0], mask_right, aux_send.at[7], aux_recv.at[7], gx, to_left)]

    def up_copy(k):
        return remote(
            modes_in.at[:, k, high - 1, :, last, :], ext.at[:, k, :, last, :], up_send.at[k], low_recv.at[k], up, gy
        )

    def up_relay(k):
        return remote(
            modes_in.at[:, k, high - 1, :, last, :], relay.at[k, :, :, first, :], up_send.at[k], relay_recv.at[k], down, gy
        )

    def down_copy(k):
        return remote(
            modes_in.at[:, k, 0, :, first, :], ext.at[:, k, :, end, :], down_send.at[k], high_recv.at[k], down, gy
        )

    def down_relay(k):
        return remote(
            modes_in.at[:, k, 0, :, first, :], relay.at[k, :, :, first, :], down_send.at[k], relay_recv.at[k], up, gy
        )

    def pass_up(k):
        return remote(
            relay.at[k, :, :, first, :], ext.at[:, k, :, last, :], pass_send.at[k], low_recv.at[k], up_two, gy
        )

    def pass_down(k):
        return remote(
            relay.at[k, :, :, first, :], ext.at[:, k, :, end, :], pass_send.at[k], high_recv.at[k], down_two, gy
        )

    def right_copy(k):
        return remote(modes_in.at[:, k, :, wide - 1], left.at[:, k], right_send.at[k], left_recv.at[k], gx, to_right)

    def left_copy(k):
        return remote(modes_in.at[:, k, :, 0], right.at[:, k], left_send.at[k], right_recv.at[k], gx, to_left)

    mean_up = remote(
        mean_in.at[:, high - 1, :, last, :], ext_mean.at[0, :, :, last, :], mean_send.at[0], mean_recv.at[0], up, gy
    )
    mean_down = remote(
        mean_in.at[:, 0, :, first, :], ext_mean.at[0, :, :, end, :], mean_send.at[1], mean_recv.at[1], down, gy
    )
    mean_right = remote(mean_in.at[:, :, wide - 1], left_mean.at[0], mean_send.at[2], mean_recv.at[2], gx, to_right)
    mean_left = remote(mean_in.at[:, :, 0], right_mean.at[0], mean_send.at[3], mean_recv.at[3], gx, to_left)

    def turn(k):
        return lax.rem(k, half)

    def send_x_level(k, carry):
        @pl.when(turn(k) < up_turns)
        def _():
            up_relay(k).start()

        @pl.when(turn(k) < down_turns)
        def _():
            down_relay(k).start()

        @pl.when(has_up & (turn(k) >= up_turns))
        def _():
            up_copy(k).start()

        @pl.when(has_down & (turn(k) >= down_turns))
        def _():
            down_copy(k).start()

        return carry

    def pass_level(k):
        @pl.when(turn(k) < pass_up_turns)
        def _():
            up_relay(k).wait_recv()
            pass_up(k).start()

        @pl.when(turn(k) < pass_down_turns)
        def _():
            down_relay(k).wait_recv()
            pass_down(k).start()

    pl.semaphore_wait(barrier, sum(there.astype(jnp.int32) for there, x, y in beside))

    @pl.when(has_up)
    def _():
        for copy in aux_up:
            copy.start()

    @pl.when(has_down)
    def _():
        for copy in aux_down:
            copy.start()

    lax.fori_loop(0, levels, send_x_level, 0)

    @pl.when(has_right)
    def _():
        for copy in aux_right:
            copy.start()

    @pl.when(has_left)
    def _():
        for copy in aux_left:
            copy.start()

    def load_and_send(k, carry):
        for copy in load_level(k):
            copy.start()

        @pl.when(has_right)
        def _():
            right_copy(k).start()

        @pl.when(has_left)
        def _():
            left_copy(k).start()

        return carry

    for copy in plane_loads:
        copy.start()

    lax.fori_loop(0, levels, load_and_send, 0)
    for there, copy in ((has_up, mean_up), (has_down, mean_down), (has_right, mean_right), (has_left, mean_left)):

        @pl.when(there)
        def _():
            copy.start()

    def zero_low(k, carry):
        for t in range(wide):
            ext[:, k, t, :SUB, :] = jnp.zeros((count, SUB, LANES), jnp.float32)
            ext_mean[:, k, t, :SUB, :] = jnp.zeros((1, SUB, LANES), jnp.float32)
        return carry

    def zero_high(k, carry):
        for t in range(wide):
            ext[:, k, t, SUB + size_x :, :] = jnp.zeros((count, SUB, LANES), jnp.float32)
            ext_mean[:, k, t, SUB + size_x :, :] = jnp.zeros((1, SUB, LANES), jnp.float32)
        return carry

    def zero_left(k, carry):
        left[:, k] = jnp.zeros((count, high, SUB, LANES), jnp.float32)
        left_mean[:, k] = jnp.zeros((1, high, SUB, LANES), jnp.float32)
        return carry

    def zero_right(k, carry):
        right[:, k] = jnp.zeros((count, high, SUB, LANES), jnp.float32)
        right_mean[:, k] = jnp.zeros((1, high, SUB, LANES), jnp.float32)
        return carry

    @pl.when(~has_down)
    def _():
        lax.fori_loop(0, levels, zero_low, 0)
        for ref in (east_low, flag_low, mask_low):
            ref[...] = jnp.zeros_like(ref)

    @pl.when(~has_up)
    def _():
        lax.fori_loop(0, levels, zero_high, 0)
        mask_high[...] = jnp.zeros_like(mask_high)

    @pl.when(~has_left)
    def _():
        lax.fori_loop(0, levels, zero_left, 0)
        for ref in (north_left, flag_left, mask_left):
            ref[...] = jnp.zeros_like(ref)

    @pl.when(~has_right)
    def _():
        lax.fori_loop(0, levels, zero_right, 0)
        mask_right[...] = jnp.zeros_like(mask_right)

    total[...] = jnp.zeros_like(total)

    for copy in plane_loads:
        copy.wait()

    for copy in load_level(0):
        copy.wait()

    for k in range(min(AHEAD, levels)):
        pass_level(k)

    @pl.when(has_down)
    def _():
        for copy in aux_up:
            copy.wait_recv()

    @pl.when(has_up)
    def _():
        for copy in aux_down:
            copy.wait_recv()

    @pl.when(has_left)
    def _():
        for copy in aux_right:
            copy.wait_recv()

    @pl.when(has_right)
    def _():
        for copy in aux_left:
            copy.wait_recv()

    lane = lax.broadcasted_iota(jnp.int32, (SUB, LANES), 1)

    def plane(ref, k):
        return jnp.concatenate(
            [jnp.concatenate([f32(ref[k, h, t]) for t in range(wide)], axis=1) for h in range(high)], axis=0
        )

    def edge_row(ref, k, row):
        return jnp.concatenate([f32(ref[k, t, row : row + 1, :]) for t in range(wide)], axis=1)

    def edge_column(ref, k, column):
        return jnp.concatenate([f32(ref[k, h])[:, column : column + 1] for h in range(high)], axis=0)

    def level_coefs(k):
        wet = plane(mask, k)
        dx = stencil(
            plane(east, k), plane(flag_east, k), wet,
            edge_row(east_low, k, SUB - 1), edge_row(flag_low, k, SUB - 1), edge_row(mask_low, k, SUB - 1),
            edge_row(mask_high, k, 0), 0,
        )
        dy = stencil(
            plane(north, k), plane(flag_north, k), wet,
            edge_column(north_left, k, LANES - 1), edge_column(flag_left, k, LANES - 1),
            edge_column(mask_left, k, LANES - 1), edge_column(mask_right, k, 0), 1,
        )
        upright = vert_diff * wet
        return [dx[s] for s in SHIFTS] + [dy[s] for s in SHIFTS] + [dx[0] + dy[0] - 2.0 * upright, upright]

    def moved(row, s):
        if s < 0:
            mixed = jnp.where(lane >= LANES + s, row[0], row[1])
        else:
            mixed = jnp.where(lane < s, row[2], row[1])
        return pltpu.roll(mixed, (-s) % LANES, 1)

    def tendency(weights, f, k, h, t, cells, beside_left, beside_right):
        above = jnp.minimum(k + 1, levels - 1)
        below = jnp.maximum(k - 1, 0)
        base = SUB + SUB * h
        cut = slice(base, base + SUB)
        c = cells[f, k, t, cut, :]
        before = cells[f, k, t - 1, cut, :] if t > 0 else beside_left[f, k, h]
        after = cells[f, k, t + 1, cut, :] if t < wide - 1 else beside_right[f, k, h]
        row = [before, c, after]
        value = weights[12] * c + weights[13] * (cells[f, above, t, cut, :] + cells[f, below, t, cut, :])
        for i, s in enumerate(SHIFTS):
            value += weights[i] * cells[f, k, t, base + s : base + s + SUB, :]
            value += weights[6 + i] * moved(row, s)
        return value

    contract = (((1,), (1,)), ((), ()))
    chains = (
        (lax.div(gx * levels, nx), 0, has_up, has_down, up, gy),
        (lax.div((nx - 1 - gx) * levels, nx), 1, has_down, has_up, down, gy),
        (lax.div(gy * levels, ny), 2, has_right, has_left, gx, to_right),
        (lax.div((ny - 1 - gy) * levels, ny), 3, has_left, has_right, gx, to_left),
    )

    def split(values):
        coarse = values.astype(jnp.bfloat16)
        return coarse, (values - f32(coarse)).astype(jnp.bfloat16)

    def level(k, carry):
        @pl.when(k + AHEAD < levels)
        def _():
            pass_level(k + AHEAD)

        for spot, forth, there, here, x, y in chains:

            @pl.when(k == spot)
            def _():
                @pl.when(here)
                def _():
                    pl.semaphore_wait(chain.at[forth], 1)

                @pl.when(there)
                def _():
                    pl.semaphore_signal(chain.at[forth], inc=1, device_id=(x, y), device_id_type=MESH)

        @pl.when(k + 1 < levels)
        def _():
            for copy in load_level(k + 1):
                copy.wait()

        for i, value in enumerate(level_coefs(k)):
            coefs[k, i] = value

        @pl.when(has_left)
        def _():
            right_copy(k).wait_recv()

        @pl.when(has_right)
        def _():
            left_copy(k).wait_recv()

        @pl.when(has_down)
        def _():
            up_copy(k).wait_recv()

        @pl.when(has_up)
        def _():
            down_copy(k).wait_recv()

        for h in range(high):
            for t in range(wide):
                weights = [
                    coefs[k, i, SUB * h : SUB * (h + 1), LANES * t : LANES * (t + 1)] for i in range(len(SHIFTS) * 2 + 2)
                ]
                for f in range(count):
                    tend[k, h * wide + t, SUB * f : SUB * (f + 1), :] = tendency(
                        weights, f, k, h, t, ext, left, right
                    )
        u = jnp.concatenate(
            [
                ext[:, k, t, SUB + SUB * h : SUB + SUB * (h + 1), :].reshape(count * SUB, LANES)
                for h in range(high)
                for t in range(wide)
            ],
            axis=1,
        )
        v = jnp.concatenate([tend[k, i] for i in range(high * wide)], axis=1)
        coarse, fine = split(jnp.concatenate([u, v], axis=0))
        total[...] += lax.dot_general(
            jnp.concatenate([coarse, fine], axis=0), coarse, contract, preferred_element_type=jnp.float32
        )
        return carry

    lax.fori_loop(0, levels, level, 0)

    def copy_y(k, slot):
        return remote(mine, along_y.at[slot], send_y.at[k], recv_y.at[slot], gx, next_y(k))

    def copy_x(k, slot):
        return remote(middle, along_x.at[slot], send_x.at[k], recv_x.at[slot], next_x(k), gy)

    tall = 2 * count * SUB
    row = lax.broadcasted_iota(jnp.int32, (tall, tall), 0)
    col = lax.broadcasted_iota(jnp.int32, (tall, tall), 1)
    cross = total[tall:, :]
    summed = jnp.where((row % SUB) == (col % SUB), total[:tall, :] + cross + cross.T, 0.0)
    pick = f32(
        lax.broadcasted_iota(jnp.int32, (2 * count, tall), 1) // SUB
        == lax.broadcasted_iota(jnp.int32, (2 * count, tall), 0)
    )
    height, width = gram.shape
    spread = f32(
        lax.broadcasted_iota(jnp.int32, (tall, width), 0) // SUB
        == lax.broadcasted_iota(jnp.int32, (tall, width), 1) % (2 * count)
    )
    part = jnp.dot(pick, summed, precision=HIGHEST, preferred_element_type=jnp.float32)
    full = jnp.dot(part, spread, precision=HIGHEST, preferred_element_type=jnp.float32)
    block = lax.broadcasted_iota(jnp.int32, gram.shape, 1) // (2 * count)
    packed = full[:height]
    for b in range(1, 2 * count // height):
        packed = jnp.where(block == b, full[b * height : (b + 1) * height], packed)
    mine[...] = packed
    along_y[gy] = packed
    for k in range(1, ny):
        copy_y(k, gy).start()
    for k in range(1, ny):
        copy_y(k, next_y(k)).wait_recv()
    summed = along_y[0]
    for k in range(1, ny):
        summed = summed + along_y[k]
    middle[...] = summed
    along_x[gx] = summed
    for k in range(1, nx):
        copy_x(k, gx).start()

    @pl.when(has_down)
    def _():
        mean_up.wait_recv()

    @pl.when(has_up)
    def _():
        mean_down.wait_recv()

    @pl.when(has_left)
    def _():
        mean_right.wait_recv()

    @pl.when(has_right)
    def _():
        mean_left.wait_recv()

    def mean_level(k, carry):
        for h in range(high):
            for t in range(wide):
                weights = [
                    coefs[k, i, SUB * h : SUB * (h + 1), LANES * t : LANES * (t + 1)] for i in range(len(SHIFTS) * 2 + 2)
                ]
                value = tendency(weights, 0, k, h, t, ext_mean, left_mean, right_mean)
                mean_next[k, h, t] = ext_mean[0, k, t, SUB + SUB * h : SUB + SUB * (h + 1), :] + time_step * value
        return carry

    lax.fori_loop(0, levels, mean_level, 0)

    for k in range(1, nx):
        copy_x(k, next_x(k)).wait_recv()
    summed = along_x[0]
    for k in range(1, nx):
        summed = summed + along_x[k]
    gram[...] = summed

    for k in range(1, ny):
        copy_y(k, gy).wait_send()
    for k in range(1, nx):
        copy_x(k, gx).wait_send()

    def settle(k, carry):
        @pl.when(has_up)
        def _():
            up_copy(k).wait_send()

        @pl.when(has_down)
        def _():
            down_copy(k).wait_send()

        @pl.when((turn(k) < pass_down_turns) | (turn(k) < pass_up_turns))
        def _():
            pass_down(k).wait_send()

        @pl.when(has_right)
        def _():
            right_copy(k).wait_send()

        @pl.when(has_left)
        def _():
            left_copy(k).wait_send()

        return carry

    lax.fori_loop(0, levels, settle, 0)
    for there, copies in (
        (has_up, aux_up + [mean_up]),
        (has_down, aux_down + [mean_down]),
        (has_right, aux_right + [mean_right]),
        (has_left, aux_left + [mean_left]),
    ):

        @pl.when(there)
        def _():
            for copy in copies:
                copy.wait_send()


def solve(packed, count, cells):
    two = 2 * count
    height, width = packed.shape
    block = lax.broadcasted_iota(jnp.int32, packed.shape, 1) // two
    stacked = jnp.concatenate([jnp.where(block == b, packed, 0.0) for b in range(two // height)], axis=0)
    fold = (
        lax.broadcasted_iota(jnp.int32, (width, two), 0) % two == lax.broadcasted_iota(jnp.int32, (width, two), 1)
    ).astype(jnp.float32)
    total = jnp.dot(stacked, fold, precision=HIGHEST, preferred_element_type=jnp.float32) / cells
    row = lax.broadcasted_iota(jnp.int32, (count, two), 0)
    col = lax.broadcasted_iota(jnp.int32, (count, two), 1)
    contract = (((1,), (1,)), ((), ()))
    update = jnp.where(
        col < count,
        jnp.where(col == row, 1.0, 0.0) - time_step * total[count:, :],
        jnp.where(col == row + count, time_step, 0.0),
    )
    padding = jnp.zeros((count, two), jnp.float32)
    halfway = jnp.dot(update, total, precision=HIGHEST, preferred_element_type=jnp.float32)
    work = lax.dot_general(
        halfway,
        jnp.concatenate([update, padding], axis=0),
        contract,
        precision=HIGHEST,
        preferred_element_type=jnp.float32,
    )
    work = work + jnp.where(col == row + count, 1.0, 0.0)
    for j in range(count):
        column = jnp.broadcast_to(work[:, j : j + 1], (count, two))
        scale = lax.rsqrt(column[j : j + 1, :])
        pivot_row = work[j : j + 1, :] * scale
        work = jnp.where(row > j, work - (column * scale) * pivot_row, jnp.where(row == j, pivot_row, work))
    factor = jnp.where(col >= row, work, 0.0)[:, :count]
    inverse = jnp.where(col >= count, work, 0.0)
    mix = jnp.dot(
        inverse,
        jnp.concatenate([padding, update], axis=0),
        precision=HIGHEST,
        preferred_element_type=jnp.float32,
    )
    return factor, mix


def combine_kernel(cells, ext, tend, mean, packed, out, mean_out, factor, result, weights, mean_sem, out_sem):
    count, levels, wide, tall, _ = ext.shape
    high = tall // SUB - 2
    tall, both_tall = count * SUB, 2 * count * SUB

    def store(k):
        return pltpu.make_async_copy(result.at[:, k], out.at[:, k], out_sem.at[k])

    store_mean = pltpu.make_async_copy(mean, mean_out, mean_sem)
    store_mean.start()
    factor[...], mix = solve(packed[...], count, cells)
    spread = (
        lax.broadcasted_iota(jnp.int32, (tall, count), 0) // SUB == lax.broadcasted_iota(jnp.int32, (tall, count), 1)
    ).astype(jnp.float32)
    along = (
        lax.broadcasted_iota(jnp.int32, (2 * count, both_tall), 1) // SUB
        == lax.broadcasted_iota(jnp.int32, (2 * count, both_tall), 0)
    ).astype(jnp.float32)
    whole = jnp.dot(
        jnp.dot(spread, mix, precision=HIGHEST, preferred_element_type=jnp.float32),
        along,
        precision=HIGHEST,
        preferred_element_type=jnp.float32,
    )
    row = lax.broadcasted_iota(jnp.int32, (tall, both_tall), 0)
    col = lax.broadcasted_iota(jnp.int32, (tall, both_tall), 1)
    whole = jnp.where((row % SUB) == (col % SUB), whole, 0.0)
    coarse = whole.astype(jnp.bfloat16)
    weights[:tall, :] = coarse
    weights[tall:, :] = (whole - coarse.astype(jnp.float32)).astype(jnp.bfloat16)

    def level(k, carry):
        both = jnp.concatenate(
            [
                jnp.concatenate(
                    [
                        ext[:, k, t, SUB + SUB * h : SUB + SUB * (h + 1), :].reshape(tall, LANES),
                        tend[k, h * wide + t],
                    ],
                    axis=0,
                )
                for h in range(high)
                for t in range(wide)
            ],
            axis=1,
        )
        coarse = both.astype(jnp.bfloat16)
        fine = (both - coarse.astype(jnp.float32)).astype(jnp.bfloat16)
        main = jnp.dot(weights[...], coarse, preferred_element_type=jnp.float32)
        mixed = main[:tall] + (main[tall:] + jnp.dot(weights[:tall, :], fine, preferred_element_type=jnp.float32))
        for h in range(high):
            for t in range(wide):
                i = h * wide + t
                result[:, k, h, t] = mixed[:, LANES * i : LANES * (i + 1)].reshape(count, SUB, LANES)
        store(k).start()
        return carry

    lax.fori_loop(0, levels, level, 0)

    def settle(k, carry):
        store(k).wait()
        return carry

    lax.fori_loop(0, levels, settle, 0)
    store_mean.wait()


def section(mean_field, mode_fields, velocity_east, velocity_north, flag_east, flag_north, ocean_mask):
    count, levels, size_x, size_y = mode_fields.shape
    nx, ny = lax.axis_size("gx"), lax.axis_size("gy")
    high, wide = size_x // SUB, size_y // LANES
    real, whole = jnp.float32, jnp.int32
    anywhere = pl.BlockSpec(memory_space=pl.ANY)
    vmem = pl.BlockSpec(memory_space=pltpu.VMEM)
    modes = blocked(mode_fields)
    planes = [blocked(a) for a in (mean_field, velocity_east, velocity_north, flag_east, flag_north, ocean_mask)]
    plane = (levels, high, wide, SUB, LANES)
    tall = 2 * count * SUB
    packed = (4 * count * count // LANES, LANES)
    spots = len(SHIFTS) * 2 + 2
    dma = pltpu.SemaphoreType.DMA
    edge_row, edge_side = (levels, wide, SUB, LANES), (levels, high, SUB, LANES)
    ext, tend, mean_next, gram = pl.pallas_call(
        functools.partial(tend_kernel, nx, ny),
        in_specs=[pl.BlockSpec(memory_space=pltpu.HBM)] * 7,
        out_specs=[vmem] * 4,
        out_shape=[
            pltpu.VMEM((count, levels, wide, size_x + 2 * SUB, LANES), real),
            pltpu.VMEM((levels, high * wide, count * SUB, LANES), real),
            pltpu.VMEM(plane, real),
            pltpu.VMEM(packed, real),
        ],
        scratch_shapes=[
            pltpu.VMEM((count, levels, high, SUB, LANES), real),
            pltpu.VMEM((count, levels, high, SUB, LANES), real),
            pltpu.VMEM((1, levels, wide, size_x + 2 * SUB, LANES), real),
            pltpu.VMEM((1, levels, high, SUB, LANES), real),
            pltpu.VMEM((1, levels, high, SUB, LANES), real),
            pltpu.VMEM((levels, count, wide, SUB, LANES), real),
            pltpu.VMEM(plane, real),
            pltpu.VMEM(plane, real),
            pltpu.VMEM(plane, whole),
            pltpu.VMEM(plane, whole),
            pltpu.VMEM(plane, whole),
            pltpu.VMEM(edge_row, real),
            pltpu.VMEM(edge_row, whole),
            pltpu.VMEM(edge_row, whole),
            pltpu.VMEM(edge_row, whole),
            pltpu.VMEM(edge_side, real),
            pltpu.VMEM(edge_side, whole),
            pltpu.VMEM(edge_side, whole),
            pltpu.VMEM(edge_side, whole),
            pltpu.VMEM((levels, spots, size_x, size_y), real),
            pltpu.VMEM((2 * tall, tall), real),
            pltpu.VMEM(packed, real),
            pltpu.VMEM(packed, real),
            pltpu.VMEM((ny,) + packed, real),
            pltpu.VMEM((nx,) + packed, real),
            dma((levels, high)),
            dma((5 + high,)),
        ]
        + [dma((levels,))] * 10
        + [dma((8,)), dma((8,)), dma((4,)), dma((4,)), pltpu.SemaphoreType.REGULAR((4,)), dma((ny,)), dma((ny,)), dma((nx,)), dma((nx,))],
        compiler_params=pltpu.CompilerParams(collective_id=0, has_side_effects=True, vmem_limit_bytes=24 << 20),
        cost_estimate=pl.CostEstimate(flops=60 * mode_fields.size, bytes_accessed=12 * mode_fields.size, transcendentals=0),
    )(*[pltpu.with_memory_space_constraint(a, pltpu.HBM) for a in (modes, *planes)])

    cell_count = float(levels * size_x * size_y * nx * ny)
    modes_next, mean_next, factor = pl.pallas_call(
        functools.partial(combine_kernel, cell_count),
        in_specs=[vmem] * 4,
        out_specs=[anywhere, anywhere, vmem],
        out_shape=[
            jax.ShapeDtypeStruct(modes.shape, real),
            jax.ShapeDtypeStruct(plane, real),
            jax.ShapeDtypeStruct((count, count), real),
        ],
        scratch_shapes=[
            pltpu.VMEM(modes.shape, real),
            pltpu.VMEM((tall, tall), jnp.bfloat16),
            dma,
            dma((levels,)),
        ],
        compiler_params=pltpu.CompilerParams(vmem_limit_bytes=12 << 20),
    )(ext, tend, mean_next, gram)
    return unblocked(mean_next), unblocked(modes_next), factor


def solution(mesh):
    grid = P(None, "gx", "gy")
    modes = P(None, None, "gx", "gy")
    return jax.shard_map(
        section,
        mesh=mesh,
        in_specs=(grid, modes, grid, grid, grid, grid, grid),
        out_specs=(grid, modes, P()),
        check_vma=False,
    )
```

```python
import functools

import jax
import jax.numpy as jnp
from jax import lax
from jax.experimental import pallas as pl
from jax.experimental.pallas import tpu as pltpu
from jax.sharding import PartitionSpec as P

time_step = 0.1
horiz_diff = 0.05
vert_diff = 0.2
HALO = 3
LANES = 128
SUB = 8
AHEAD = 4
HIGHEST = lax.Precision.HIGHEST
MESH = pl.DeviceIdType.MESH
SHIFTS = (-3, -2, -1, 1, 2, 3)


def blocked(array):
    *lead, size_x, size_y = array.shape
    at = len(lead)
    return jnp.swapaxes(array.reshape(*lead, size_x // SUB, SUB, size_y // LANES, LANES), at + 1, at + 2)


def unblocked(array):
    *lead, high, wide, sub, lanes = array.shape
    at = len(lead)
    return jnp.swapaxes(array, at + 1, at + 2).reshape(*lead, high * sub, wide * lanes)


def face_weights(pos, neg, openness):
    return {
        -2: openness * (2.0 * pos) / 60.0,
        -1: openness * (-13.0 * pos - 3.0 * neg) / 60.0,
        0: openness * ((47.0 * pos + 27.0 * neg) / 60.0 + horiz_diff),
        1: openness * ((27.0 * pos + 47.0 * neg) / 60.0 - horiz_diff),
        2: openness * (-3.0 * pos - 13.0 * neg) / 60.0,
        3: openness * (2.0 * neg) / 60.0,
    }


def stencil(speed, side, cells, speed_before, side_before, cells_before, cells_after, axis):
    size = cells.shape[axis]
    spot = lax.broadcasted_iota(jnp.int32, cells.shape, axis)
    beyond = jnp.where(spot == size - 1, cells_after, pltpu.roll(cells, size - 1, axis))
    face = face_weights(speed * side, speed * (1.0 - side), cells * beyond)
    first = cells[:1, :] if axis == 0 else cells[:, :1]
    entry = face_weights(speed_before * side_before, speed_before * (1.0 - side_before), cells_before * first)
    result = {}
    for s in range(-3, 4):
        value = 0.0
        if s + 1 in face:
            value = value + jnp.where(spot == 0, entry[s + 1], pltpu.roll(face[s + 1], 1, axis))
        if s in face:
            value = value - face[s]
        result[s] = cells * value
    return result


def f32(value):
    return value.astype(jnp.float32)


def tend_kernel(
    nx, ny,
    modes_in, mean_in, east_in, north_in, flag_east_in, flag_north_in, mask_in,
    ext, tend, mean_next, gram,
    left, right, ext_mean, left_mean, right_mean, relay,
    east, north, flag_east, flag_north, mask,
    east_low, flag_low, mask_low, mask_high,
    north_left, flag_left, mask_left, mask_right,
    coefs, total, low, high_side, mine, middle, along_y, along_x,
    load_sem, plane_sem, up_send, down_send, pass_send, low_recv, high_recv, relay_recv,
    right_send, left_send, left_recv, right_recv,
    aux_send, aux_recv, mean_send, mean_recv, chain, send_y, recv_y, send_x, recv_x,
):
    count, levels, high, wide, _, _ = modes_in.shape
    size_x, size_y = high * SUB, wide * LANES
    gx, gy = lax.axis_index("gx"), lax.axis_index("gy")
    half = nx // 2
    odd = lax.rem(gx, 2)
    pair = lax.div(gx, 2)
    has_up, has_down = gx < nx - 1, gx > 0
    has_right, has_left = gy < ny - 1, gy > 0
    up, down = jnp.minimum(gx + 1, nx - 1), jnp.maximum(gx - 1, 0)
    up_two, down_two = jnp.minimum(gx + 2, nx - 1), jnp.maximum(gx - 2, 0)
    to_right, to_left = jnp.minimum(gy + 1, ny - 1), jnp.maximum(gy - 1, 0)
    up_turns = jnp.where(odd == 1, half - 1 - pair, 0)
    down_turns = jnp.where(odd == 0, pair, 0)
    pass_down_turns = jnp.where(odd == 1, pair, 0)
    pass_up_turns = jnp.where(odd == 0, half - 1 - pair, 0)
    barrier = pltpu.get_barrier_semaphore()

    def next_y(k):
        return lax.rem(gy + k, ny)

    def next_x(k):
        return lax.rem(gx + k, nx)

    beside = (
        (has_up, up, gy),
        (has_down, down, gy),
        (gx < nx - 2, up_two, gy),
        (gx > 1, down_two, gy),
        (has_right, gx, to_right),
        (has_left, gx, to_left),
    )
    for there, x, y in beside:

        @pl.when(there)
        def _():
            pl.semaphore_signal(barrier, inc=1, device_id=(x, y), device_id_type=MESH)

    def remote(src, dst, send, recv, x, y):
        return pltpu.make_async_remote_copy(
            src_ref=src, dst_ref=dst, send_sem=send, recv_sem=recv, device_id=(x, y), device_id_type=MESH
        )

    def load_level(k):
        return [
            pltpu.make_async_copy(
                modes_in.at[:, k, h], ext.at[:, k, :, pl.ds(SUB + SUB * h, SUB), :], load_sem.at[k, h]
            )
            for h in range(high)
        ]

    plane_loads = [
        pltpu.make_async_copy(src, dst, plane_sem.at[i])
        for i, (src, dst) in enumerate(
            [(east_in, east), (flag_east_in, flag_east), (mask_in, mask), (north_in, north), (flag_north_in, flag_north)]
        )
    ] + [
        pltpu.make_async_copy(mean_in.at[:, h], ext_mean.at[0, :, :, pl.ds(SUB + SUB * h, SUB), :], plane_sem.at[5 + h])
        for h in range(high)
    ]

    last, first = pl.ds(SUB - HALO, HALO), pl.ds(0, HALO)
    end = pl.ds(SUB + size_x, HALO)
    start = pl.ds(SUB, HALO)
    last_row = pl.ds(SUB - 1, 1)
    first_row = pl.ds(0, 1)

    aux_up = [
        remote(src.at[:, high - 1, :, last_row, :], dst.at[:, :, last_row, :], aux_send.at[i], aux_recv.at[i], up, gy)
        for i, (src, dst) in enumerate([(east_in, east_low), (flag_east_in, flag_low), (mask_in, mask_low)])
    ]
    aux_down = [
        remote(mask_in.at[:, 0, :, first_row, :], mask_high.at[:, :, first_row, :], aux_send.at[3], aux_recv.at[3], down, gy)
    ]
    aux_right = [
        remote(src.at[:, :, wide - 1], dst, aux_send.at[4 + i], aux_recv.at[4 + i], gx, to_right)
        for i, (src, dst) in enumerate([(north_in, north_left), (flag_north_in, flag_left), (mask_in, mask_left)])
    ]
    aux_left = [remote(mask_in.at[:, :, 0], mask_right, aux_send.at[7], aux_recv.at[7], gx, to_left)]

    def up_copy(k):
        return remote(
            modes_in.at[:, k, high - 1, :, last, :], low.at[:, k, :, last, :], up_send.at[k], low_recv.at[k], up, gy
        )

    def up_relay(k):
        return remote(
            modes_in.at[:, k, high - 1, :, last, :], relay.at[k, :, :, first, :], up_send.at[k], relay_recv.at[k], down, gy
        )

    def down_copy(k):
        return remote(
            modes_in.at[:, k, 0, :, first, :], high_side.at[:, k, :, start, :], down_send.at[k], high_recv.at[k], down, gy
        )

    def down_relay(k):
        return remote(
            modes_in.at[:, k, 0, :, first, :], relay.at[k, :, :, first, :], down_send.at[k], relay_recv.at[k], up, gy
        )

    def pass_up(k):
        return remote(
            relay.at[k, :, :, first, :], low.at[:, k, :, last, :], pass_send.at[k], low_recv.at[k], up_two, gy
        )

    def pass_down(k):
        return remote(
            relay.at[k, :, :, first, :], high_side.at[:, k, :, start, :], pass_send.at[k], high_recv.at[k], down_two, gy
        )

    def right_copy(k):
        return remote(modes_in.at[:, k, :, wide - 1], left.at[:, k], right_send.at[k], left_recv.at[k], gx, to_right)

    def left_copy(k):
        return remote(modes_in.at[:, k, :, 0], right.at[:, k], left_send.at[k], right_recv.at[k], gx, to_left)

    mean_up = remote(
        mean_in.at[:, high - 1, :, last, :], ext_mean.at[0, :, :, last, :], mean_send.at[0], mean_recv.at[0], up, gy
    )
    mean_down = remote(
        mean_in.at[:, 0, :, first, :], ext_mean.at[0, :, :, end, :], mean_send.at[1], mean_recv.at[1], down, gy
    )
    mean_right = remote(mean_in.at[:, :, wide - 1], left_mean.at[0], mean_send.at[2], mean_recv.at[2], gx, to_right)
    mean_left = remote(mean_in.at[:, :, 0], right_mean.at[0], mean_send.at[3], mean_recv.at[3], gx, to_left)

    def turn(k):
        return lax.rem(k, half)

    def send_relayed(k, carry):
        @pl.when(turn(k) < up_turns)
        def _():
            up_relay(k).start()

        @pl.when(turn(k) < down_turns)
        def _():
            down_relay(k).start()

        return carry

    def send_x_level(k, carry):
        @pl.when(has_up & (turn(k) >= up_turns))
        def _():
            up_copy(k).start()

        @pl.when(has_down & (turn(k) >= down_turns))
        def _():
            down_copy(k).start()

        return carry

    def pass_level(k):
        @pl.when(turn(k) < pass_up_turns)
        def _():
            up_relay(k).wait_recv()
            pass_up(k).start()

        @pl.when(turn(k) < pass_down_turns)
        def _():
            down_relay(k).wait_recv()
            pass_down(k).start()

    pl.semaphore_wait(barrier, sum(there.astype(jnp.int32) for there, x, y in beside))

    @pl.when(has_up)
    def _():
        for copy in aux_up:
            copy.start()

    @pl.when(has_down)
    def _():
        for copy in aux_down:
            copy.start()

    lax.fori_loop(0, levels, send_relayed, 0)
    lax.fori_loop(0, levels, send_x_level, 0)

    @pl.when(has_right)
    def _():
        for copy in aux_right:
            copy.start()

    @pl.when(has_left)
    def _():
        for copy in aux_left:
            copy.start()

    def load_and_send(k, carry):
        for copy in load_level(k):
            copy.start()

        @pl.when(has_right)
        def _():
            right_copy(k).start()

        @pl.when(has_left)
        def _():
            left_copy(k).start()

        return carry

    for copy in plane_loads:
        copy.start()

    lax.fori_loop(0, levels, load_and_send, 0)
    for there, copy in ((has_up, mean_up), (has_down, mean_down), (has_right, mean_right), (has_left, mean_left)):

        @pl.when(there)
        def _():
            copy.start()

    nothing = jnp.zeros((count, SUB, LANES), jnp.float32)

    def zero_beyond(k, carry):
        for t in range(wide):
            ext[:, k, t, :SUB, :] = nothing
            ext[:, k, t, SUB + size_x :, :] = nothing
            low[:, k, t, SUB:, :] = nothing
            high_side[:, k, t, :SUB, :] = nothing
        return carry

    lax.fori_loop(0, levels, zero_beyond, 0)

    def zero_low(k, carry):
        for t in range(wide):
            low[:, k, t, :SUB, :] = nothing
            ext_mean[:, k, t, :SUB, :] = jnp.zeros((1, SUB, LANES), jnp.float32)
        return carry

    def zero_high(k, carry):
        for t in range(wide):
            high_side[:, k, t, SUB:, :] = nothing
            ext_mean[:, k, t, SUB + size_x :, :] = jnp.zeros((1, SUB, LANES), jnp.float32)
        return carry

    def zero_left(k, carry):
        left[:, k] = jnp.zeros((count, high, SUB, LANES), jnp.float32)
        left_mean[:, k] = jnp.zeros((1, high, SUB, LANES), jnp.float32)
        return carry

    def zero_right(k, carry):
        right[:, k] = jnp.zeros((count, high, SUB, LANES), jnp.float32)
        right_mean[:, k] = jnp.zeros((1, high, SUB, LANES), jnp.float32)
        return carry

    @pl.when(~has_down)
    def _():
        lax.fori_loop(0, levels, zero_low, 0)
        for ref in (east_low, flag_low, mask_low):
            ref[...] = jnp.zeros_like(ref)

    @pl.when(~has_up)
    def _():
        lax.fori_loop(0, levels, zero_high, 0)
        mask_high[...] = jnp.zeros_like(mask_high)

    @pl.when(~has_left)
    def _():
        lax.fori_loop(0, levels, zero_left, 0)
        for ref in (north_left, flag_left, mask_left):
            ref[...] = jnp.zeros_like(ref)

    @pl.when(~has_right)
    def _():
        lax.fori_loop(0, levels, zero_right, 0)
        mask_right[...] = jnp.zeros_like(mask_right)

    total[...] = jnp.zeros_like(total)

    for copy in plane_loads:
        copy.wait()

    for k in range(min(2, levels)):
        for copy in load_level(k):
            copy.wait()

    for k in range(min(AHEAD, levels)):
        pass_level(k)

    @pl.when(has_down)
    def _():
        for copy in aux_up:
            copy.wait_recv()

    @pl.when(has_up)
    def _():
        for copy in aux_down:
            copy.wait_recv()

    @pl.when(has_left)
    def _():
        for copy in aux_right:
            copy.wait_recv()

    @pl.when(has_right)
    def _():
        for copy in aux_left:
            copy.wait_recv()

    lane = lax.broadcasted_iota(jnp.int32, (SUB, LANES), 1)

    def plane(ref, k):
        return jnp.concatenate(
            [jnp.concatenate([f32(ref[k, h, t]) for t in range(wide)], axis=1) for h in range(high)], axis=0
        )

    def edge_row(ref, k, row):
        return jnp.concatenate([f32(ref[k, t, row : row + 1, :]) for t in range(wide)], axis=1)

    def edge_column(ref, k, column):
        return jnp.concatenate([f32(ref[k, h])[:, column : column + 1] for h in range(high)], axis=0)

    def level_coefs(k):
        wet = plane(mask, k)
        dx = stencil(
            plane(east, k), plane(flag_east, k), wet,
            edge_row(east_low, k, SUB - 1), edge_row(flag_low, k, SUB - 1), edge_row(mask_low, k, SUB - 1),
            edge_row(mask_high, k, 0), 0,
        )
        dy = stencil(
            plane(north, k), plane(flag_north, k), wet,
            edge_column(north_left, k, LANES - 1), edge_column(flag_left, k, LANES - 1),
            edge_column(mask_left, k, LANES - 1), edge_column(mask_right, k, 0), 1,
        )
        upright = vert_diff * wet
        return [dx[s] for s in SHIFTS] + [dy[s] for s in SHIFTS] + [dx[0] + dy[0] - 2.0 * upright, upright]

    def moved(row, s):
        if s < 0:
            mixed = jnp.where(lane >= LANES + s, row[0], row[1])
        else:
            mixed = jnp.where(lane < s, row[2], row[1])
        return pltpu.roll(mixed, (-s) % LANES, 1)

    def tendency(weights, f, k, h, t, cells, beside_left, beside_right):
        above = jnp.minimum(k + 1, levels - 1)
        below = jnp.maximum(k - 1, 0)
        base = SUB + SUB * h
        cut = slice(base, base + SUB)
        c = cells[f, k, t, cut, :]
        before = cells[f, k, t - 1, cut, :] if t > 0 else beside_left[f, k, h]
        after = cells[f, k, t + 1, cut, :] if t < wide - 1 else beside_right[f, k, h]
        row = [before, c, after]
        value = weights[12] * c + weights[13] * (cells[f, above, t, cut, :] + cells[f, below, t, cut, :])
        for i, s in enumerate(SHIFTS):
            value += weights[i] * cells[f, k, t, base + s : base + s + SUB, :]
            value += weights[6 + i] * moved(row, s)
        return value

    contract = (((1,), (1,)), ((), ()))
    chains = (
        (lax.div(gx * levels, nx), 0, has_up, has_down, up, gy),
        (lax.div((nx - 1 - gx) * levels, nx), 1, has_down, has_up, down, gy),
        (lax.div(gy * levels, ny), 2, has_right, has_left, gx, to_right),
        (lax.div((ny - 1 - gy) * levels, ny), 3, has_left, has_right, gx, to_left),
    )

    def split(values):
        coarse = values.astype(jnp.bfloat16)
        return coarse, (values - f32(coarse)).astype(jnp.bfloat16)

    def inner_tendency(k):
        for i, value in enumerate(level_coefs(k)):
            coefs[k, i] = value

        @pl.when(has_left)
        def _():
            right_copy(k).wait_recv()

        @pl.when(has_right)
        def _():
            left_copy(k).wait_recv()

        for h in range(high):
            for t in range(wide):
                weights = [
                    coefs[k, i, SUB * h : SUB * (h + 1), LANES * t : LANES * (t + 1)] for i in range(len(SHIFTS) * 2 + 2)
                ]
                for f in range(count):
                    tend[k, h * wide + t, SUB * f : SUB * (f + 1), :] = tendency(
                        weights, f, k, h, t, ext, left, right
                    )

    def level(k, carry):
        @pl.when(k + AHEAD < levels)
        def _():
            pass_level(k + AHEAD)

        for spot, forth, there, here, x, y in chains:

            @pl.when(k == spot)
            def _():
                @pl.when(here)
                def _():
                    pl.semaphore_wait(chain.at[forth], 1)

                @pl.when(there)
                def _():
                    pl.semaphore_signal(chain.at[forth], inc=1, device_id=(x, y), device_id_type=MESH)

        @pl.when(k + 2 < levels)
        def _():
            for copy in load_level(k + 2):
                copy.wait()

        @pl.when(k + 1 < levels)
        def _():
            inner_tendency(k + 1)

        @pl.when(has_down)
        def _():
            up_copy(k).wait_recv()

        @pl.when(has_up)
        def _():
            down_copy(k).wait_recv()

        for h, side, taps in ((0, low, (0, 1, 2)), (high - 1, high_side, (3, 4, 5))):
            for t in range(wide):
                edge = [
                    coefs[k, i, SUB * h : SUB * (h + 1), LANES * t : LANES * (t + 1)] for i in range(len(SHIFTS))
                ]
                for f in range(count):
                    cut = slice(SUB * f, SUB * (f + 1))
                    value = tend[k, h * wide + t, cut, :]
                    for i in taps:
                        base = SHIFTS[i] + (SUB if i < HALO else 0)
                        value += edge[i] * side[f, k, t, base : base + SUB, :]
                    tend[k, h * wide + t, cut, :] = value
        u = jnp.concatenate(
            [
                ext[:, k, t, SUB + SUB * h : SUB + SUB * (h + 1), :].reshape(count * SUB, LANES)
                for h in range(high)
                for t in range(wide)
            ],
            axis=1,
        )
        v = jnp.concatenate([tend[k, i] for i in range(high * wide)], axis=1)
        coarse, fine = split(jnp.concatenate([u, v], axis=0))
        total[...] += lax.dot_general(
            jnp.concatenate([coarse, fine], axis=0), coarse, contract, preferred_element_type=jnp.float32
        )
        return carry

    inner_tendency(0)
    lax.fori_loop(0, levels, level, 0)

    def copy_y(k, slot):
        return remote(mine, along_y.at[slot], send_y.at[k], recv_y.at[slot], gx, next_y(k))

    def copy_x(k, slot):
        return remote(middle, along_x.at[slot], send_x.at[k], recv_x.at[slot], next_x(k), gy)

    two, tall = 2 * count, 2 * count * SUB

    def thirds(values, axis):
        coarse = values.astype(jnp.bfloat16)
        rest = values - f32(coarse)
        middling = rest.astype(jnp.bfloat16)
        return jnp.concatenate([coarse, middling, (rest - f32(middling)).astype(jnp.bfloat16)], axis=axis)

    def group(shape, axis):
        return lax.rem(lax.broadcasted_iota(jnp.int32, shape, axis), tall) // SUB

    kept = (lax.broadcasted_iota(jnp.int32, (tall, tall), 0) % SUB) == (
        lax.broadcasted_iota(jnp.int32, (tall, tall), 1) % SUB
    )
    pick = (
        group((two, 3 * tall), 1) == lax.broadcasted_iota(jnp.int32, (two, 3 * tall), 0)
    ).astype(jnp.bfloat16)
    spread = (
        group((3 * tall, two), 0) == lax.broadcasted_iota(jnp.int32, (3 * tall, two), 1)
    ).astype(jnp.bfloat16)
    picked = jnp.concatenate(
        [
            jnp.dot(pick, thirds(jnp.where(kept, part, 0.0), 0), preferred_element_type=jnp.float32)
            for part in (total[:tall, :], total[tall:, :])
        ],
        axis=0,
    )
    both = jnp.dot(thirds(picked, 1), spread, preferred_element_type=jnp.float32)
    cross = both[two:, :]
    summed = both[:two, :] + cross + cross.T
    height = gram.shape[0]
    packed = jnp.concatenate([summed[height * b : height * (b + 1), :] for b in range(two // height)], axis=1)
    mine[...] = packed
    along_y[gy] = packed
    for k in range(1, ny):
        copy_y(k, gy).start()
    for k in range(1, ny):
        copy_y(k, next_y(k)).wait_recv()
    summed = along_y[0]
    for k in range(1, ny):
        summed = summed + along_y[k]
    middle[...] = summed
    along_x[gx] = summed
    for k in range(1, nx):
        copy_x(k, gx).start()

    @pl.when(has_down)
    def _():
        mean_up.wait_recv()

    @pl.when(has_up)
    def _():
        mean_down.wait_recv()

    @pl.when(has_left)
    def _():
        mean_right.wait_recv()

    @pl.when(has_right)
    def _():
        mean_left.wait_recv()

    def mean_level(k, carry):
        for h in range(high):
            for t in range(wide):
                weights = [
                    coefs[k, i, SUB * h : SUB * (h + 1), LANES * t : LANES * (t + 1)] for i in range(len(SHIFTS) * 2 + 2)
                ]
                value = tendency(weights, 0, k, h, t, ext_mean, left_mean, right_mean)
                mean_next[k, h, t] = ext_mean[0, k, t, SUB + SUB * h : SUB + SUB * (h + 1), :] + time_step * value
        return carry

    lax.fori_loop(0, levels, mean_level, 0)

    def settle(k, carry):
        @pl.when(has_up)
        def _():
            up_copy(k).wait_send()

        @pl.when(has_down)
        def _():
            down_copy(k).wait_send()

        @pl.when((turn(k) < pass_down_turns) | (turn(k) < pass_up_turns))
        def _():
            pass_down(k).wait_send()

        @pl.when(has_right)
        def _():
            right_copy(k).wait_send()

        @pl.when(has_left)
        def _():
            left_copy(k).wait_send()

        return carry

    lax.fori_loop(0, levels, settle, 0)
    for there, copies in (
        (has_up, aux_up + [mean_up]),
        (has_down, aux_down + [mean_down]),
        (has_right, aux_right + [mean_right]),
        (has_left, aux_left + [mean_left]),
    ):

        @pl.when(there)
        def _():
            for copy in copies:
                copy.wait_send()

    for k in range(1, ny):
        copy_y(k, gy).wait_send()
    for k in range(1, nx):
        copy_x(k, next_x(k)).wait_recv()
    summed = along_x[0]
    for k in range(1, nx):
        summed = summed + along_x[k]
    gram[...] = summed

    for k in range(1, nx):
        copy_x(k, gx).wait_send()


def solve(packed, count, cells):
    two = 2 * count
    total = jnp.concatenate([packed[:, two * b : two * (b + 1)] for b in range(two // packed.shape[0])], axis=0) / cells
    row = lax.broadcasted_iota(jnp.int32, (count, two), 0)
    col = lax.broadcasted_iota(jnp.int32, (count, two), 1)
    contract = (((1,), (1,)), ((), ()))
    update = jnp.where(
        col < count,
        jnp.where(col == row, 1.0, 0.0) - time_step * total[count:, :],
        jnp.where(col == row + count, time_step, 0.0),
    )
    padding = jnp.zeros((count, two), jnp.float32)
    halfway = jnp.dot(update, total, precision=HIGHEST, preferred_element_type=jnp.float32)
    work = lax.dot_general(
        halfway,
        jnp.concatenate([update, padding], axis=0),
        contract,
        precision=HIGHEST,
        preferred_element_type=jnp.float32,
    )
    work = work + jnp.where(col == row + count, 1.0, 0.0)
    for j in range(count):
        column = jnp.broadcast_to(work[:, j : j + 1], (count, two))
        scale = lax.rsqrt(column[j : j + 1, :])
        pivot_row = work[j : j + 1, :] * scale
        work = jnp.where(row > j, work - (column * scale) * pivot_row, jnp.where(row == j, pivot_row, work))
    factor = jnp.where(col >= row, work, 0.0)[:, :count]
    inverse = jnp.where(col >= count, work, 0.0)
    mix = jnp.dot(
        inverse,
        jnp.concatenate([padding, update], axis=0),
        precision=HIGHEST,
        preferred_element_type=jnp.float32,
    )
    return factor, mix


def combine_kernel(cells, ext, tend, mean, packed, out, mean_out, factor, result, weights, mean_sem, out_sem):
    count, levels, wide, tall, _ = ext.shape
    high = tall // SUB - 2
    tall, both_tall = count * SUB, 2 * count * SUB

    def store(k):
        return pltpu.make_async_copy(result.at[:, k], out.at[:, k], out_sem.at[k])

    store_mean = pltpu.make_async_copy(mean, mean_out, mean_sem)
    store_mean.start()
    factor[...], mix = solve(packed[...], count, cells)
    coarse = mix.astype(jnp.bfloat16)
    halves = jnp.concatenate([f32(coarse), mix - f32(coarse)], axis=0).astype(jnp.bfloat16)
    spread = (
        lax.broadcasted_iota(jnp.int32, (both_tall, 2 * count), 0) // SUB
        == lax.broadcasted_iota(jnp.int32, (both_tall, 2 * count), 1)
    ).astype(jnp.bfloat16)
    along = (
        lax.broadcasted_iota(jnp.int32, (2 * count, both_tall), 1) // SUB
        == lax.broadcasted_iota(jnp.int32, (2 * count, both_tall), 0)
    ).astype(jnp.bfloat16)
    tall_halves = jnp.dot(spread, halves, preferred_element_type=jnp.float32).astype(jnp.bfloat16)
    whole = jnp.dot(tall_halves, along, preferred_element_type=jnp.float32)
    row = lax.broadcasted_iota(jnp.int32, (both_tall, both_tall), 0)
    col = lax.broadcasted_iota(jnp.int32, (both_tall, both_tall), 1)
    weights[...] = jnp.where((row % SUB) == (col % SUB), whole, 0.0).astype(jnp.bfloat16)

    def level(k, carry):
        both = jnp.concatenate(
            [
                jnp.concatenate(
                    [
                        ext[:, k, t, SUB + SUB * h : SUB + SUB * (h + 1), :].reshape(tall, LANES),
                        tend[k, h * wide + t],
                    ],
                    axis=0,
                )
                for h in range(high)
                for t in range(wide)
            ],
            axis=1,
        )
        coarse = both.astype(jnp.bfloat16)
        fine = (both - coarse.astype(jnp.float32)).astype(jnp.bfloat16)
        main = jnp.dot(weights[...], coarse, preferred_element_type=jnp.float32)
        mixed = main[:tall] + (main[tall:] + jnp.dot(weights[:tall, :], fine, preferred_element_type=jnp.float32))
        for h in range(high):
            for t in range(wide):
                i = h * wide + t
                result[:, k, h, t] = mixed[:, LANES * i : LANES * (i + 1)].reshape(count, SUB, LANES)
        store(k).start()
        return carry

    lax.fori_loop(0, levels, level, 0, unroll=4)

    def settle(k, carry):
        store(k).wait()
        return carry

    lax.fori_loop(0, levels, settle, 0)
    store_mean.wait()


def section(mean_field, mode_fields, velocity_east, velocity_north, flag_east, flag_north, ocean_mask):
    count, levels, size_x, size_y = mode_fields.shape
    nx, ny = lax.axis_size("gx"), lax.axis_size("gy")
    high, wide = size_x // SUB, size_y // LANES
    real, whole = jnp.float32, jnp.int32
    anywhere = pl.BlockSpec(memory_space=pl.ANY)
    vmem = pl.BlockSpec(memory_space=pltpu.VMEM)
    modes = blocked(mode_fields)
    planes = [blocked(a) for a in (mean_field, velocity_east, velocity_north, flag_east, flag_north, ocean_mask)]
    plane = (levels, high, wide, SUB, LANES)
    tall = 2 * count * SUB
    packed = (4 * count * count // LANES, LANES)
    spots = len(SHIFTS) * 2 + 2
    dma = pltpu.SemaphoreType.DMA
    edge_row, edge_side = (levels, wide, SUB, LANES), (levels, high, SUB, LANES)
    ext, tend, mean_next, gram = pl.pallas_call(
        functools.partial(tend_kernel, nx, ny),
        in_specs=[pl.BlockSpec(memory_space=pltpu.HBM)] * 7,
        out_specs=[vmem] * 4,
        out_shape=[
            pltpu.VMEM((count, levels, wide, size_x + 2 * SUB, LANES), real),
            pltpu.VMEM((levels, high * wide, count * SUB, LANES), real),
            pltpu.VMEM(plane, real),
            pltpu.VMEM(packed, real),
        ],
        scratch_shapes=[
            pltpu.VMEM((count, levels, high, SUB, LANES), real),
            pltpu.VMEM((count, levels, high, SUB, LANES), real),
            pltpu.VMEM((1, levels, wide, size_x + 2 * SUB, LANES), real),
            pltpu.VMEM((1, levels, high, SUB, LANES), real),
            pltpu.VMEM((1, levels, high, SUB, LANES), real),
            pltpu.VMEM((levels, count, wide, SUB, LANES), real),
            pltpu.VMEM(plane, real),
            pltpu.VMEM(plane, real),
            pltpu.VMEM(plane, whole),
            pltpu.VMEM(plane, whole),
            pltpu.VMEM(plane, whole),
            pltpu.VMEM(edge_row, real),
            pltpu.VMEM(edge_row, whole),
            pltpu.VMEM(edge_row, whole),
            pltpu.VMEM(edge_row, whole),
            pltpu.VMEM(edge_side, real),
            pltpu.VMEM(edge_side, whole),
            pltpu.VMEM(edge_side, whole),
            pltpu.VMEM(edge_side, whole),
            pltpu.VMEM((levels, spots, size_x, size_y), real),
            pltpu.VMEM((2 * tall, tall), real),
            pltpu.VMEM((count, levels, wide, 2 * SUB, LANES), real),
            pltpu.VMEM((count, levels, wide, 2 * SUB, LANES), real),
            pltpu.VMEM(packed, real),
            pltpu.VMEM(packed, real),
            pltpu.VMEM((ny,) + packed, real),
            pltpu.VMEM((nx,) + packed, real),
            dma((levels, high)),
            dma((5 + high,)),
        ]
        + [dma((levels,))] * 10
        + [dma((8,)), dma((8,)), dma((4,)), dma((4,)), pltpu.SemaphoreType.REGULAR((4,)), dma((ny,)), dma((ny,)), dma((nx,)), dma((nx,))],
        compiler_params=pltpu.CompilerParams(collective_id=0, has_side_effects=True, vmem_limit_bytes=32 << 20),
        cost_estimate=pl.CostEstimate(flops=60 * mode_fields.size, bytes_accessed=12 * mode_fields.size, transcendentals=0),
    )(*[pltpu.with_memory_space_constraint(a, pltpu.HBM) for a in (modes, *planes)])

    cell_count = float(levels * size_x * size_y * nx * ny)
    modes_next, mean_next, factor = pl.pallas_call(
        functools.partial(combine_kernel, cell_count),
        in_specs=[vmem] * 4,
        out_specs=[anywhere, anywhere, vmem],
        out_shape=[
            jax.ShapeDtypeStruct(modes.shape, real),
            jax.ShapeDtypeStruct(plane, real),
            jax.ShapeDtypeStruct((count, count), real),
        ],
        scratch_shapes=[
            pltpu.VMEM(modes.shape, real),
            pltpu.VMEM((tall, tall), jnp.bfloat16),
            dma,
            dma((levels,)),
        ],
        compiler_params=pltpu.CompilerParams(vmem_limit_bytes=12 << 20),
    )(ext, tend, mean_next, gram)
    return unblocked(mean_next), unblocked(modes_next), factor


def solution(mesh):
    grid = P(None, "gx", "gy")
    modes = P(None, None, "gx", "gy")
    return jax.shard_map(
        section,
        mesh=mesh,
        in_specs=(grid, modes, grid, grid, grid, grid, grid),
        out_specs=(grid, modes, P()),
        check_vma=False,
    )
```

```python
import functools

import jax
import jax.numpy as jnp
from jax import lax
from jax.experimental import pallas as pl
from jax.experimental.pallas import tpu as pltpu
from jax.sharding import PartitionSpec as P

time_step = 0.1
horiz_diff = 0.05
vert_diff = 0.2
HALO = 3
LANES = 128
SUB = 8
AHEAD = 4
BLOCK = 4
HIGHEST = lax.Precision.HIGHEST
MESH = pl.DeviceIdType.MESH
SHIFTS = (-3, -2, -1, 1, 2, 3)


def blocked(array):
    *lead, size_x, size_y = array.shape
    at = len(lead)
    return jnp.swapaxes(array.reshape(*lead, size_x // SUB, SUB, size_y // LANES, LANES), at + 1, at + 2)


def unblocked(array):
    *lead, high, wide, sub, lanes = array.shape
    at = len(lead)
    return jnp.swapaxes(array, at + 1, at + 2).reshape(*lead, high * sub, wide * lanes)


def face_weights(pos, neg, openness):
    return {
        -2: openness * (2.0 * pos) / 60.0,
        -1: openness * (-13.0 * pos - 3.0 * neg) / 60.0,
        0: openness * ((47.0 * pos + 27.0 * neg) / 60.0 + horiz_diff),
        1: openness * ((27.0 * pos + 47.0 * neg) / 60.0 - horiz_diff),
        2: openness * (-3.0 * pos - 13.0 * neg) / 60.0,
        3: openness * (2.0 * neg) / 60.0,
    }


def stencil(speed, side, cells, speed_before, side_before, cells_before, cells_after, axis):
    size = cells.shape[axis]
    spot = lax.broadcasted_iota(jnp.int32, cells.shape, axis)
    beyond = jnp.where(spot == size - 1, cells_after, pltpu.roll(cells, size - 1, axis))
    face = face_weights(speed * side, speed * (1.0 - side), cells * beyond)
    first = cells[:1, :] if axis == 0 else cells[:, :1]
    entry = face_weights(speed_before * side_before, speed_before * (1.0 - side_before), cells_before * first)
    result = {}
    for s in range(-3, 4):
        value = 0.0
        if s + 1 in face:
            value = value + jnp.where(spot == 0, entry[s + 1], pltpu.roll(face[s + 1], 1, axis))
        if s in face:
            value = value - face[s]
        result[s] = cells * value
    return result


def doublings(first, size):
    steps = []
    while first < size - 1:
        steps.append(first)
        first *= 2
    return steps


def f32(value):
    return value.astype(jnp.float32)


def tend_kernel(
    nx, ny,
    modes_in, mean_in, east_in, north_in, flag_east_in, flag_north_in, mask_in,
    ext, tend, mean_next, gram,
    left, right, ext_mean, left_mean, right_mean, relay,
    east, north, flag_east, flag_north, mask,
    east_low, flag_low, mask_low, mask_high,
    north_left, flag_left, mask_left, mask_right,
    coefs, total, low, high_side, mine, slots,
    load_sem, plane_sem, up_send, down_send, pass_send, low_recv, high_recv, relay_recv,
    right_send, left_send, left_recv, right_recv,
    aux_send, aux_recv, mean_send, mean_recv, known, part_send, part_recv,
):
    count, levels, high, wide, _, _ = modes_in.shape
    size_x, size_y = high * SUB, wide * LANES
    gx, gy = lax.axis_index("gx"), lax.axis_index("gy")
    half = nx // 2
    odd = lax.rem(gx, 2)
    pair = lax.div(gx, 2)
    has_up, has_down = gx < nx - 1, gx > 0
    has_right, has_left = gy < ny - 1, gy > 0
    up, down = jnp.minimum(gx + 1, nx - 1), jnp.maximum(gx - 1, 0)
    up_two, down_two = jnp.minimum(gx + 2, nx - 1), jnp.maximum(gx - 2, 0)
    to_right, to_left = jnp.minimum(gy + 1, ny - 1), jnp.maximum(gy - 1, 0)
    up_turns = jnp.where(odd == 1, half - 1 - pair, 0)
    down_turns = jnp.where(odd == 0, pair, 0)
    pass_down_turns = jnp.where(odd == 1, pair, 0)
    pass_up_turns = jnp.where(odd == 0, half - 1 - pair, 0)
    barrier = pltpu.get_barrier_semaphore()

    def next_y(k):
        return lax.rem(gy + k, ny)

    def next_x(k):
        return lax.rem(gx + k, nx)

    beside = (
        (has_up, up, gy),
        (has_down, down, gy),
        (gx < nx - 2, up_two, gy),
        (gx > 1, down_two, gy),
        (has_right, gx, to_right),
        (has_left, gx, to_left),
    )
    for there, x, y in beside:

        @pl.when(there)
        def _():
            pl.semaphore_signal(barrier, inc=1, device_id=(x, y), device_id_type=MESH)

    def remote(src, dst, send, recv, x, y):
        return pltpu.make_async_remote_copy(
            src_ref=src, dst_ref=dst, send_sem=send, recv_sem=recv, device_id=(x, y), device_id_type=MESH
        )

    def load_level(k):
        return [
            pltpu.make_async_copy(
                modes_in.at[:, k, h], ext.at[:, k, :, pl.ds(SUB + SUB * h, SUB), :], load_sem.at[k, h]
            )
            for h in range(high)
        ]

    plane_loads = [
        pltpu.make_async_copy(src, dst, plane_sem.at[i])
        for i, (src, dst) in enumerate(
            [(east_in, east), (flag_east_in, flag_east), (mask_in, mask), (north_in, north), (flag_north_in, flag_north)]
        )
    ] + [
        pltpu.make_async_copy(mean_in.at[:, h], ext_mean.at[0, :, :, pl.ds(SUB + SUB * h, SUB), :], plane_sem.at[5 + h])
        for h in range(high)
    ]

    last, first = pl.ds(SUB - HALO, HALO), pl.ds(0, HALO)
    end = pl.ds(SUB + size_x, HALO)
    start = pl.ds(SUB, HALO)
    last_row = pl.ds(SUB - 1, 1)
    first_row = pl.ds(0, 1)

    aux_up = [
        remote(src.at[:, high - 1, :, last_row, :], dst.at[:, :, last_row, :], aux_send.at[i], aux_recv.at[i], up, gy)
        for i, (src, dst) in enumerate([(east_in, east_low), (flag_east_in, flag_low), (mask_in, mask_low)])
    ]
    aux_down = [
        remote(mask_in.at[:, 0, :, first_row, :], mask_high.at[:, :, first_row, :], aux_send.at[3], aux_recv.at[3], down, gy)
    ]
    aux_right = [
        remote(src.at[:, :, wide - 1], dst, aux_send.at[4 + i], aux_recv.at[4 + i], gx, to_right)
        for i, (src, dst) in enumerate([(north_in, north_left), (flag_north_in, flag_left), (mask_in, mask_left)])
    ]
    aux_left = [remote(mask_in.at[:, :, 0], mask_right, aux_send.at[7], aux_recv.at[7], gx, to_left)]

    def up_copy(k):
        return remote(
            modes_in.at[:, k, high - 1, :, last, :], low.at[:, k, :, last, :], up_send.at[k], low_recv.at[k], up, gy
        )

    def up_relay(k):
        return remote(
            modes_in.at[:, k, high - 1, :, last, :], relay.at[k, :, :, first, :], up_send.at[k], relay_recv.at[k], down, gy
        )

    def down_copy(k):
        return remote(
            modes_in.at[:, k, 0, :, first, :], high_side.at[:, k, :, start, :], down_send.at[k], high_recv.at[k], down, gy
        )

    def down_relay(k):
        return remote(
            modes_in.at[:, k, 0, :, first, :], relay.at[k, :, :, first, :], down_send.at[k], relay_recv.at[k], up, gy
        )

    def pass_up(k):
        return remote(
            relay.at[k, :, :, first, :], low.at[:, k, :, last, :], pass_send.at[k], low_recv.at[k], up_two, gy
        )

    def pass_down(k):
        return remote(
            relay.at[k, :, :, first, :], high_side.at[:, k, :, start, :], pass_send.at[k], high_recv.at[k], down_two, gy
        )

    def right_copy(k):
        return remote(modes_in.at[:, k, :, wide - 1], left.at[:, k], right_send.at[k], left_recv.at[k], gx, to_right)

    def left_copy(k):
        return remote(modes_in.at[:, k, :, 0], right.at[:, k], left_send.at[k], right_recv.at[k], gx, to_left)

    mean_up = remote(
        mean_in.at[:, high - 1, :, last, :], ext_mean.at[0, :, :, last, :], mean_send.at[0], mean_recv.at[0], up, gy
    )
    mean_down = remote(
        mean_in.at[:, 0, :, first, :], ext_mean.at[0, :, :, end, :], mean_send.at[1], mean_recv.at[1], down, gy
    )
    mean_right = remote(mean_in.at[:, :, wide - 1], left_mean.at[0], mean_send.at[2], mean_recv.at[2], gx, to_right)
    mean_left = remote(mean_in.at[:, :, 0], right_mean.at[0], mean_send.at[3], mean_recv.at[3], gx, to_left)

    def turn(k):
        return lax.rem(k, half)

    def send_relayed(k, carry):
        @pl.when(turn(k) < up_turns)
        def _():
            up_relay(k).start()

        @pl.when(turn(k) < down_turns)
        def _():
            down_relay(k).start()

        return carry

    def send_x_level(k, carry):
        @pl.when(has_up & (turn(k) >= up_turns))
        def _():
            up_copy(k).start()

        @pl.when(has_down & (turn(k) >= down_turns))
        def _():
            down_copy(k).start()

        return carry

    def pass_level(k):
        @pl.when(turn(k) < pass_up_turns)
        def _():
            up_relay(k).wait_recv()
            pass_up(k).start()

        @pl.when(turn(k) < pass_down_turns)
        def _():
            down_relay(k).wait_recv()
            pass_down(k).start()

    pl.semaphore_wait(barrier, sum(there.astype(jnp.int32) for there, x, y in beside))

    @pl.when(has_up)
    def _():
        for copy in aux_up:
            copy.start()

    @pl.when(has_down)
    def _():
        for copy in aux_down:
            copy.start()

    lax.fori_loop(0, levels, send_relayed, 0)
    lax.fori_loop(0, levels, send_x_level, 0)

    @pl.when(has_right)
    def _():
        for copy in aux_right:
            copy.start()

    @pl.when(has_left)
    def _():
        for copy in aux_left:
            copy.start()

    def load_and_send(k, carry):
        for copy in load_level(k):
            copy.start()

        @pl.when(has_right)
        def _():
            right_copy(k).start()

        @pl.when(has_left)
        def _():
            left_copy(k).start()

        return carry

    for copy in plane_loads:
        copy.start()

    lax.fori_loop(0, levels, load_and_send, 0)
    for there, copy in ((has_up, mean_up), (has_down, mean_down), (has_right, mean_right), (has_left, mean_left)):

        @pl.when(there)
        def _():
            copy.start()

    nothing = jnp.zeros((count, SUB, LANES), jnp.float32)

    def zero_beyond(k, carry):
        for t in range(wide):
            ext[:, k, t, :SUB, :] = nothing
            ext[:, k, t, SUB + size_x :, :] = nothing
            low[:, k, t, SUB:, :] = nothing
            high_side[:, k, t, :SUB, :] = nothing
        return carry

    lax.fori_loop(0, levels, zero_beyond, 0)

    def zero_low(k, carry):
        for t in range(wide):
            low[:, k, t, :SUB, :] = nothing
            ext_mean[:, k, t, :SUB, :] = jnp.zeros((1, SUB, LANES), jnp.float32)
        return carry

    def zero_high(k, carry):
        for t in range(wide):
            high_side[:, k, t, SUB:, :] = nothing
            ext_mean[:, k, t, SUB + size_x :, :] = jnp.zeros((1, SUB, LANES), jnp.float32)
        return carry

    def zero_left(k, carry):
        left[:, k] = jnp.zeros((count, high, SUB, LANES), jnp.float32)
        left_mean[:, k] = jnp.zeros((1, high, SUB, LANES), jnp.float32)
        return carry

    def zero_right(k, carry):
        right[:, k] = jnp.zeros((count, high, SUB, LANES), jnp.float32)
        right_mean[:, k] = jnp.zeros((1, high, SUB, LANES), jnp.float32)
        return carry

    @pl.when(~has_down)
    def _():
        lax.fori_loop(0, levels, zero_low, 0)
        for ref in (east_low, flag_low, mask_low):
            ref[...] = jnp.zeros_like(ref)

    @pl.when(~has_up)
    def _():
        lax.fori_loop(0, levels, zero_high, 0)
        mask_high[...] = jnp.zeros_like(mask_high)

    @pl.when(~has_left)
    def _():
        lax.fori_loop(0, levels, zero_left, 0)
        for ref in (north_left, flag_left, mask_left):
            ref[...] = jnp.zeros_like(ref)

    @pl.when(~has_right)
    def _():
        lax.fori_loop(0, levels, zero_right, 0)
        mask_right[...] = jnp.zeros_like(mask_right)

    total[...] = jnp.zeros_like(total)

    for copy in plane_loads:
        copy.wait()

    for k in range(min(2, levels)):
        for copy in load_level(k):
            copy.wait()

    for k in range(min(AHEAD, levels)):
        pass_level(k)

    @pl.when(has_down)
    def _():
        for copy in aux_up:
            copy.wait_recv()

    @pl.when(has_up)
    def _():
        for copy in aux_down:
            copy.wait_recv()

    @pl.when(has_left)
    def _():
        for copy in aux_right:
            copy.wait_recv()

    @pl.when(has_right)
    def _():
        for copy in aux_left:
            copy.wait_recv()

    lane = lax.broadcasted_iota(jnp.int32, (SUB, LANES), 1)

    def plane(ref, k):
        return jnp.concatenate(
            [jnp.concatenate([f32(ref[k, h, t]) for t in range(wide)], axis=1) for h in range(high)], axis=0
        )

    def edge_row(ref, k, row):
        return jnp.concatenate([f32(ref[k, t, row : row + 1, :]) for t in range(wide)], axis=1)

    def edge_column(ref, k, column):
        return jnp.concatenate([f32(ref[k, h])[:, column : column + 1] for h in range(high)], axis=0)

    def level_coefs(k):
        wet = plane(mask, k)
        dx = stencil(
            plane(east, k), plane(flag_east, k), wet,
            edge_row(east_low, k, SUB - 1), edge_row(flag_low, k, SUB - 1), edge_row(mask_low, k, SUB - 1),
            edge_row(mask_high, k, 0), 0,
        )
        dy = stencil(
            plane(north, k), plane(flag_north, k), wet,
            edge_column(north_left, k, LANES - 1), edge_column(flag_left, k, LANES - 1),
            edge_column(mask_left, k, LANES - 1), edge_column(mask_right, k, 0), 1,
        )
        upright = vert_diff * wet
        return [dx[s] for s in SHIFTS] + [dy[s] for s in SHIFTS] + [dx[0] + dy[0] - 2.0 * upright, upright]

    def moved(row, s):
        if s < 0:
            mixed = jnp.where(lane >= LANES + s, row[0], row[1])
        else:
            mixed = jnp.where(lane < s, row[2], row[1])
        return pltpu.roll(mixed, (-s) % LANES, 1)

    def tendency(weights, f, k, h, t, cells, beside_left, beside_right):
        above = jnp.minimum(k + 1, levels - 1)
        below = jnp.maximum(k - 1, 0)
        base = SUB + SUB * h
        cut = slice(base, base + SUB)
        c = cells[f, k, t, cut, :]
        before = cells[f, k, t - 1, cut, :] if t > 0 else beside_left[f, k, h]
        after = cells[f, k, t + 1, cut, :] if t < wide - 1 else beside_right[f, k, h]
        row = [before, c, after]
        value = weights[12] * c + weights[13] * (cells[f, above, t, cut, :] + cells[f, below, t, cut, :])
        for i, s in enumerate(SHIFTS):
            value += weights[i] * cells[f, k, t, base + s : base + s + SUB, :]
            value += weights[6 + i] * moved(row, s)
        return value

    contract = (((1,), (1,)), ((), ()))
    def along_x(step):
        return [
            (gx + step < nx, jnp.minimum(gx + step, nx - 1), gy),
            (gx >= step, jnp.maximum(gx - step, 0), gy),
        ]

    def along_y(step):
        return [
            (gy + step < ny, gx, jnp.minimum(gy + step, ny - 1)),
            (gy >= step, gx, jnp.maximum(gy - step, 0)),
        ]

    rounds = [along_y(step) for step in doublings(1, ny)]
    rounds += [along_x(1) + along_x(2)] + [along_x(step) for step in doublings(2, nx)]

    def split(values):
        coarse = values.astype(jnp.bfloat16)
        return coarse, (values - f32(coarse)).astype(jnp.bfloat16)

    def inner_tendency(k):
        for i, value in enumerate(level_coefs(k)):
            coefs[k, i] = value

        @pl.when(has_left)
        def _():
            right_copy(k).wait_recv()

        @pl.when(has_right)
        def _():
            left_copy(k).wait_recv()

        for h in range(high):
            for t in range(wide):
                weights = [
                    coefs[k, i, SUB * h : SUB * (h + 1), LANES * t : LANES * (t + 1)] for i in range(len(SHIFTS) * 2 + 2)
                ]
                for f in range(count):
                    tend[k, h * wide + t, SUB * f : SUB * (f + 1), :] = tendency(
                        weights, f, k, h, t, ext, left, right
                    )

    def level(k, carry):
        @pl.when(k + AHEAD < levels)
        def _():
            pass_level(k + AHEAD)

        for n in range(len(rounds) + 1):

            @pl.when(k == n * levels // (len(rounds) + 1))
            def _():
                if n > 0:
                    heard = sum(there.astype(jnp.int32) for there, x, y in rounds[n - 1])
                    pl.semaphore_wait(known.at[n - 1], heard)
                if n < len(rounds):
                    for there, x, y in rounds[n]:

                        @pl.when(there)
                        def _():
                            pl.semaphore_signal(known.at[n], inc=1, device_id=(x, y), device_id_type=MESH)

        @pl.when(k + 2 < levels)
        def _():
            for copy in load_level(k + 2):
                copy.wait()

        @pl.when(k + 1 < levels)
        def _():
            inner_tendency(k + 1)

        @pl.when(has_down)
        def _():
            up_copy(k).wait_recv()

        @pl.when(has_up)
        def _():
            down_copy(k).wait_recv()

        for h, side, taps in ((0, low, (0, 1, 2)), (high - 1, high_side, (3, 4, 5))):
            for t in range(wide):
                edge = [
                    coefs[k, i, SUB * h : SUB * (h + 1), LANES * t : LANES * (t + 1)] for i in range(len(SHIFTS))
                ]
                for f in range(count):
                    cut = slice(SUB * f, SUB * (f + 1))
                    value = tend[k, h * wide + t, cut, :]
                    for i in taps:
                        base = SHIFTS[i] + (SUB if i < HALO else 0)
                        value += edge[i] * side[f, k, t, base : base + SUB, :]
                    tend[k, h * wide + t, cut, :] = value
        u = jnp.concatenate(
            [
                ext[:, k, t, SUB + SUB * h : SUB + SUB * (h + 1), :].reshape(count * SUB, LANES)
                for h in range(high)
                for t in range(wide)
            ],
            axis=1,
        )
        v = jnp.concatenate([tend[k, i] for i in range(high * wide)], axis=1)
        coarse, fine = split(jnp.concatenate([u, v], axis=0))
        total[...] += lax.dot_general(
            jnp.concatenate([coarse, fine], axis=0), coarse, contract, preferred_element_type=jnp.float32
        )
        return carry

    inner_tendency(0)
    lax.fori_loop(0, levels, level, 0)

    others = [(i, j) for i in range(nx) for j in range(ny) if i or j]
    me = gx * ny + gy

    def other(step):
        return next_x(step[0]), next_y(step[1])

    def part_copy(n, slot):
        return remote(mine, slots.at[slot], part_send.at[n], part_recv.at[slot], *other(others[n]))

    two, tall = 2 * count, 2 * count * SUB

    def thirds(values, axis):
        coarse = values.astype(jnp.bfloat16)
        rest = values - f32(coarse)
        middling = rest.astype(jnp.bfloat16)
        return jnp.concatenate([coarse, middling, (rest - f32(middling)).astype(jnp.bfloat16)], axis=axis)

    def group(shape, axis):
        return lax.rem(lax.broadcasted_iota(jnp.int32, shape, axis), tall) // SUB

    kept = (lax.broadcasted_iota(jnp.int32, (tall, tall), 0) % SUB) == (
        lax.broadcasted_iota(jnp.int32, (tall, tall), 1) % SUB
    )
    pick = (
        group((two, 3 * tall), 1) == lax.broadcasted_iota(jnp.int32, (two, 3 * tall), 0)
    ).astype(jnp.bfloat16)
    spread = (
        group((3 * tall, two), 0) == lax.broadcasted_iota(jnp.int32, (3 * tall, two), 1)
    ).astype(jnp.bfloat16)
    picked = jnp.concatenate(
        [
            jnp.dot(pick, thirds(jnp.where(kept, part, 0.0), 0), preferred_element_type=jnp.float32)
            for part in (total[:tall, :], total[tall:, :])
        ],
        axis=0,
    )
    both = jnp.dot(thirds(picked, 1), spread, preferred_element_type=jnp.float32)
    cross = both[two:, :]
    summed = both[:two, :] + cross + cross.T
    row = lax.broadcasted_iota(jnp.int32, (count, count), 0)
    col = lax.broadcasted_iota(jnp.int32, (count, count), 1)
    outer = summed[count:, count:]
    kept = jnp.concatenate([jnp.where(col >= row, summed[:count, :count], outer), summed[count:, :count]], axis=1)
    height = gram.shape[0] - 1
    mine[:height, :] = jnp.concatenate([kept[height * b : height * (b + 1), :] for b in range(count // height)], axis=1)
    mine[height:, :] = jnp.concatenate(
        [
            jnp.sum(jnp.where(row == col, outer, 0.0), axis=0, keepdims=True),
            jnp.zeros((1, LANES - count), jnp.float32),
        ],
        axis=1,
    )
    slots[me] = mine[...]
    for n in range(len(others)):
        part_copy(n, me).start()

    @pl.when(has_down)
    def _():
        mean_up.wait_recv()

    @pl.when(has_up)
    def _():
        mean_down.wait_recv()

    @pl.when(has_left)
    def _():
        mean_right.wait_recv()

    @pl.when(has_right)
    def _():
        mean_left.wait_recv()

    def mean_level(k, carry):
        for h in range(high):
            for t in range(wide):
                weights = [
                    coefs[k, i, SUB * h : SUB * (h + 1), LANES * t : LANES * (t + 1)] for i in range(len(SHIFTS) * 2 + 2)
                ]
                value = tendency(weights, 0, k, h, t, ext_mean, left_mean, right_mean)
                mean_next[k, h, t] = ext_mean[0, k, t, SUB + SUB * h : SUB + SUB * (h + 1), :] + time_step * value
        return carry

    lax.fori_loop(0, levels, mean_level, 0)

    def settle(k, carry):
        @pl.when(has_up)
        def _():
            up_copy(k).wait_send()

        @pl.when(has_down)
        def _():
            down_copy(k).wait_send()

        @pl.when((turn(k) < pass_down_turns) | (turn(k) < pass_up_turns))
        def _():
            pass_down(k).wait_send()

        @pl.when(has_right)
        def _():
            right_copy(k).wait_send()

        @pl.when(has_left)
        def _():
            left_copy(k).wait_send()

        return carry

    lax.fori_loop(0, levels, settle, 0)
    for there, copies in (
        (has_up, aux_up + [mean_up]),
        (has_down, aux_down + [mean_down]),
        (has_right, aux_right + [mean_right]),
        (has_left, aux_left + [mean_left]),
    ):

        @pl.when(there)
        def _():
            for copy in copies:
                copy.wait_send()

    for n, step in enumerate(others):
        x, y = other(step)
        part_copy(n, x * ny + y).wait_recv()
    summed = slots[0]
    for n in range(1, nx * ny):
        summed = summed + slots[n]
    gram[...] = summed
    for n in range(len(others)):
        part_copy(n, me).wait_send()


def solve(packed, count, cells):
    two = 2 * count
    height = packed.shape[0] - 1
    kept = (
        jnp.concatenate([packed[:height, two * b : two * (b + 1)] for b in range(count // height)], axis=0) / cells
    )
    flipped = kept.T
    row = lax.broadcasted_iota(jnp.int32, (count, count), 0)
    col = lax.broadcasted_iota(jnp.int32, (count, count), 1)
    mixed, mirrored = kept[:, :count], flipped[:count, :]
    outer = jnp.where(row == col, packed[height:, :count] / cells, jnp.where(col < row, mixed, mirrored))
    total = jnp.concatenate(
        [
            jnp.concatenate([jnp.where(col >= row, mixed, mirrored), flipped[count:, :]], axis=1),
            jnp.concatenate([kept[:, count:], outer], axis=1),
        ],
        axis=0,
    )
    row = lax.broadcasted_iota(jnp.int32, (count, two), 0)
    col = lax.broadcasted_iota(jnp.int32, (count, two), 1)
    contract = (((1,), (1,)), ((), ()))
    update = jnp.where(
        col < count,
        jnp.where(col == row, 1.0, 0.0) - time_step * total[count:, :],
        jnp.where(col == row + count, time_step, 0.0),
    )
    padding = jnp.zeros((count, two), jnp.float32)
    halfway = jnp.dot(update, total, precision=HIGHEST, preferred_element_type=jnp.float32)
    work = lax.dot_general(
        halfway,
        jnp.concatenate([update, padding], axis=0),
        contract,
        precision=HIGHEST,
        preferred_element_type=jnp.float32,
    )
    work = work + jnp.where(col == row + count, 1.0, 0.0)
    for first in range(0, count, BLOCK):
        block = range(first, min(first + BLOCK, count))
        columns = {j: jnp.broadcast_to(work[:, j : j + 1], (count, two)) for j in block}
        for j in block:
            scale = lax.rsqrt(columns[j][j : j + 1, :])
            pivot_row = work[j : j + 1, :] * scale
            column = columns[j] * scale
            work = jnp.where(row > j, work - column * pivot_row, jnp.where(row == j, pivot_row, work))
            for m in block:
                if m > j:
                    columns[m] = columns[m] - column * column[m : m + 1, :]
    factor = jnp.where(col >= row, work, 0.0)[:, :count]
    inverse = jnp.where(col >= count, work, 0.0)
    mix = jnp.dot(
        inverse,
        jnp.concatenate([padding, update], axis=0),
        precision=HIGHEST,
        preferred_element_type=jnp.float32,
    )
    return factor, mix


def combine_kernel(cells, ext, tend, mean, packed, out, mean_out, factor, result, weights, mean_sem, out_sem):
    count, levels, wide, tall, _ = ext.shape
    high = tall // SUB - 2
    tall, both_tall = count * SUB, 2 * count * SUB

    def store(k):
        return pltpu.make_async_copy(result.at[:, k], out.at[:, k], out_sem.at[k])

    store_mean = pltpu.make_async_copy(mean, mean_out, mean_sem)
    store_mean.start()
    factor[...], mix = solve(packed[...], count, cells)
    coarse = mix.astype(jnp.bfloat16)
    halves = jnp.concatenate([f32(coarse), mix - f32(coarse)], axis=0).astype(jnp.bfloat16)
    spread = (
        lax.broadcasted_iota(jnp.int32, (both_tall, 2 * count), 0) // SUB
        == lax.broadcasted_iota(jnp.int32, (both_tall, 2 * count), 1)
    ).astype(jnp.bfloat16)
    along = (
        lax.broadcasted_iota(jnp.int32, (2 * count, both_tall), 1) // SUB
        == lax.broadcasted_iota(jnp.int32, (2 * count, both_tall), 0)
    ).astype(jnp.bfloat16)
    tall_halves = jnp.dot(spread, halves, preferred_element_type=jnp.float32).astype(jnp.bfloat16)
    whole = jnp.dot(tall_halves, along, preferred_element_type=jnp.float32)
    row = lax.broadcasted_iota(jnp.int32, (both_tall, both_tall), 0)
    col = lax.broadcasted_iota(jnp.int32, (both_tall, both_tall), 1)
    weights[...] = jnp.where((row % SUB) == (col % SUB), whole, 0.0).astype(jnp.bfloat16)

    def level(k, carry):
        both = jnp.concatenate(
            [
                jnp.concatenate(
                    [
                        ext[:, k, t, SUB + SUB * h : SUB + SUB * (h + 1), :].reshape(tall, LANES),
                        tend[k, h * wide + t],
                    ],
                    axis=0,
                )
                for h in range(high)
                for t in range(wide)
            ],
            axis=1,
        )
        coarse = both.astype(jnp.bfloat16)
        fine = (both - coarse.astype(jnp.float32)).astype(jnp.bfloat16)
        main = jnp.dot(weights[...], coarse, preferred_element_type=jnp.float32)
        mixed = main[:tall] + (main[tall:] + jnp.dot(weights[:tall, :], fine, preferred_element_type=jnp.float32))
        for h in range(high):
            for t in range(wide):
                i = h * wide + t
                result[:, k, h, t] = mixed[:, LANES * i : LANES * (i + 1)].reshape(count, SUB, LANES)
        store(k).start()
        return carry

    lax.fori_loop(0, levels, level, 0, unroll=8)

    def settle(k, carry):
        store(k).wait()
        return carry

    lax.fori_loop(0, levels, settle, 0)
    store_mean.wait()


def section(mean_field, mode_fields, velocity_east, velocity_north, flag_east, flag_north, ocean_mask):
    count, levels, size_x, size_y = mode_fields.shape
    nx, ny = lax.axis_size("gx"), lax.axis_size("gy")
    high, wide = size_x // SUB, size_y // LANES
    real, whole = jnp.float32, jnp.int32
    anywhere = pl.BlockSpec(memory_space=pl.ANY)
    vmem = pl.BlockSpec(memory_space=pltpu.VMEM)
    modes = blocked(mode_fields)
    planes = [blocked(a) for a in (mean_field, velocity_east, velocity_north, flag_east, flag_north, ocean_mask)]
    plane = (levels, high, wide, SUB, LANES)
    tall = 2 * count * SUB
    packed = (2 * count * count // LANES + 1, LANES)
    spots = len(SHIFTS) * 2 + 2
    dma = pltpu.SemaphoreType.DMA
    rounds = len(doublings(1, ny)) + 1 + len(doublings(2, nx))
    edge_row, edge_side = (levels, wide, SUB, LANES), (levels, high, SUB, LANES)
    ext, tend, mean_next, gram = pl.pallas_call(
        functools.partial(tend_kernel, nx, ny),
        in_specs=[pl.BlockSpec(memory_space=pltpu.HBM)] * 7,
        out_specs=[vmem] * 4,
        out_shape=[
            pltpu.VMEM((count, levels, wide, size_x + 2 * SUB, LANES), real),
            pltpu.VMEM((levels, high * wide, count * SUB, LANES), real),
            pltpu.VMEM(plane, real),
            pltpu.VMEM(packed, real),
        ],
        scratch_shapes=[
            pltpu.VMEM((count, levels, high, SUB, LANES), real),
            pltpu.VMEM((count, levels, high, SUB, LANES), real),
            pltpu.VMEM((1, levels, wide, size_x + 2 * SUB, LANES), real),
            pltpu.VMEM((1, levels, high, SUB, LANES), real),
            pltpu.VMEM((1, levels, high, SUB, LANES), real),
            pltpu.VMEM((levels, count, wide, SUB, LANES), real),
            pltpu.VMEM(plane, real),
            pltpu.VMEM(plane, real),
            pltpu.VMEM(plane, whole),
            pltpu.VMEM(plane, whole),
            pltpu.VMEM(plane, whole),
            pltpu.VMEM(edge_row, real),
            pltpu.VMEM(edge_row, whole),
            pltpu.VMEM(edge_row, whole),
            pltpu.VMEM(edge_row, whole),
            pltpu.VMEM(edge_side, real),
            pltpu.VMEM(edge_side, whole),
            pltpu.VMEM(edge_side, whole),
            pltpu.VMEM(edge_side, whole),
            pltpu.VMEM((levels, spots, size_x, size_y), real),
            pltpu.VMEM((2 * tall, tall), real),
            pltpu.VMEM((count, levels, wide, 2 * SUB, LANES), real),
            pltpu.VMEM((count, levels, wide, 2 * SUB, LANES), real),
            pltpu.VMEM(packed, real),
            pltpu.VMEM((nx * ny,) + packed, real),
            dma((levels, high)),
            dma((5 + high,)),
        ]
        + [dma((levels,))] * 10
        + [dma((8,)), dma((8,)), dma((4,)), dma((4,)), pltpu.SemaphoreType.REGULAR((rounds,)), dma((nx * ny - 1,)), dma((nx * ny,))],
        compiler_params=pltpu.CompilerParams(collective_id=0, has_side_effects=True, vmem_limit_bytes=32 << 20),
        cost_estimate=pl.CostEstimate(flops=60 * mode_fields.size, bytes_accessed=12 * mode_fields.size, transcendentals=0),
    )(*[pltpu.with_memory_space_constraint(a, pltpu.HBM) for a in (modes, *planes)])

    cell_count = float(levels * size_x * size_y * nx * ny)
    modes_next, mean_next, factor = pl.pallas_call(
        functools.partial(combine_kernel, cell_count),
        in_specs=[vmem] * 4,
        out_specs=[anywhere, anywhere, vmem],
        out_shape=[
            jax.ShapeDtypeStruct(modes.shape, real),
            jax.ShapeDtypeStruct(plane, real),
            jax.ShapeDtypeStruct((count, count), real),
        ],
        scratch_shapes=[
            pltpu.VMEM(modes.shape, real),
            pltpu.VMEM((tall, tall), jnp.bfloat16),
            dma,
            dma((levels,)),
        ],
        compiler_params=pltpu.CompilerParams(vmem_limit_bytes=12 << 20),
    )(ext, tend, mean_next, gram)
    return unblocked(mean_next), unblocked(modes_next), factor


def solution(mesh):
    grid = P(None, "gx", "gy")
    modes = P(None, None, "gx", "gy")
    return jax.shard_map(
        section,
        mesh=mesh,
        in_specs=(grid, modes, grid, grid, grid, grid, grid),
        out_specs=(grid, modes, P()),
        check_vma=False,
    )
```

```python
import functools

import jax
import jax.numpy as jnp
from jax import lax
from jax.experimental import pallas as pl
from jax.experimental.pallas import tpu as pltpu
from jax.sharding import PartitionSpec as P

time_step = 0.1
horiz_diff = 0.05
vert_diff = 0.2
HALO = 3
LANES = 128
SUB = 8
AHEAD = 4
BLOCK = 8
HIGHEST = lax.Precision.HIGHEST
MESH = pl.DeviceIdType.MESH
SHIFTS = (-3, -2, -1, 1, 2, 3)


def blocked(array):
    *lead, size_x, size_y = array.shape
    at = len(lead)
    return jnp.swapaxes(array.reshape(*lead, size_x // SUB, SUB, size_y // LANES, LANES), at + 1, at + 2)


def unblocked(array):
    *lead, high, wide, sub, lanes = array.shape
    at = len(lead)
    return jnp.swapaxes(array, at + 1, at + 2).reshape(*lead, high * sub, wide * lanes)


def face_weights(pos, neg, openness):
    return {
        -2: openness * (2.0 * pos) / 60.0,
        -1: openness * (-13.0 * pos - 3.0 * neg) / 60.0,
        0: openness * ((47.0 * pos + 27.0 * neg) / 60.0 + horiz_diff),
        1: openness * ((27.0 * pos + 47.0 * neg) / 60.0 - horiz_diff),
        2: openness * (-3.0 * pos - 13.0 * neg) / 60.0,
        3: openness * (2.0 * neg) / 60.0,
    }


def stencil(speed, side, cells, speed_before, side_before, cells_before, cells_after, axis):
    size = cells.shape[axis]
    spot = lax.broadcasted_iota(jnp.int32, cells.shape, axis)
    beyond = jnp.where(spot == size - 1, cells_after, pltpu.roll(cells, size - 1, axis))
    face = face_weights(speed * side, speed * (1.0 - side), cells * beyond)
    first = cells[:1, :] if axis == 0 else cells[:, :1]
    entry = face_weights(speed_before * side_before, speed_before * (1.0 - side_before), cells_before * first)
    result = {}
    for s in range(-3, 4):
        value = 0.0
        if s + 1 in face:
            value = value + jnp.where(spot == 0, entry[s + 1], pltpu.roll(face[s + 1], 1, axis))
        if s in face:
            value = value - face[s]
        result[s] = cells * value
    return result


def doublings(first, size):
    steps = []
    while first < size - 1:
        steps.append(first)
        first *= 2
    return steps


def f32(value):
    return value.astype(jnp.float32)


def tend_kernel(
    nx, ny,
    modes_in, mean_in, east_in, north_in, flag_east_in, flag_north_in, mask_in,
    ext, tend, mean_next, gram,
    left, right, ext_mean, left_mean, right_mean, relay,
    east, north, flag_east, flag_north, mask,
    east_low, flag_low, mask_low, mask_high,
    north_left, flag_left, mask_left, mask_right,
    coefs, total, low, high_side, mine, slots,
    load_sem, plane_sem, up_send, down_send, pass_send, low_recv, high_recv, relay_recv,
    right_send, left_send, left_recv, right_recv,
    aux_send, aux_recv, mean_send, mean_recv, known, part_send, part_recv,
):
    count, levels, high, wide, _, _ = modes_in.shape
    size_x, size_y = high * SUB, wide * LANES
    gx, gy = lax.axis_index("gx"), lax.axis_index("gy")
    half = nx // 2
    odd = lax.rem(gx, 2)
    pair = lax.div(gx, 2)
    has_up, has_down = gx < nx - 1, gx > 0
    has_right, has_left = gy < ny - 1, gy > 0
    up, down = jnp.minimum(gx + 1, nx - 1), jnp.maximum(gx - 1, 0)
    up_two, down_two = jnp.minimum(gx + 2, nx - 1), jnp.maximum(gx - 2, 0)
    to_right, to_left = jnp.minimum(gy + 1, ny - 1), jnp.maximum(gy - 1, 0)
    up_turns = jnp.where(odd == 1, half - 1 - pair, 0)
    down_turns = jnp.where(odd == 0, pair, 0)
    pass_down_turns = jnp.where(odd == 1, pair, 0)
    pass_up_turns = jnp.where(odd == 0, half - 1 - pair, 0)
    barrier = pltpu.get_barrier_semaphore()

    def next_y(k):
        return lax.rem(gy + k, ny)

    def next_x(k):
        return lax.rem(gx + k, nx)

    beside = (
        (has_up, up, gy),
        (has_down, down, gy),
        (gx < nx - 2, up_two, gy),
        (gx > 1, down_two, gy),
        (has_right, gx, to_right),
        (has_left, gx, to_left),
    )
    for there, x, y in beside:

        @pl.when(there)
        def _():
            pl.semaphore_signal(barrier, inc=1, device_id=(x, y), device_id_type=MESH)

    def remote(src, dst, send, recv, x, y):
        return pltpu.make_async_remote_copy(
            src_ref=src, dst_ref=dst, send_sem=send, recv_sem=recv, device_id=(x, y), device_id_type=MESH
        )

    def load_level(k):
        return [
            pltpu.make_async_copy(
                modes_in.at[:, k, h], ext.at[:, k, :, pl.ds(SUB + SUB * h, SUB), :], load_sem.at[k, h]
            )
            for h in range(high)
        ]

    plane_loads = [
        pltpu.make_async_copy(src, dst, plane_sem.at[i])
        for i, (src, dst) in enumerate(
            [(east_in, east), (flag_east_in, flag_east), (mask_in, mask), (north_in, north), (flag_north_in, flag_north)]
        )
    ] + [
        pltpu.make_async_copy(mean_in.at[:, h], ext_mean.at[0, :, :, pl.ds(SUB + SUB * h, SUB), :], plane_sem.at[5 + h])
        for h in range(high)
    ]

    last, first = pl.ds(SUB - HALO, HALO), pl.ds(0, HALO)
    end = pl.ds(SUB + size_x, HALO)
    start = pl.ds(SUB, HALO)
    last_row = pl.ds(SUB - 1, 1)
    first_row = pl.ds(0, 1)

    aux_up = [
        remote(src.at[:, high - 1, :, last_row, :], dst.at[:, :, last_row, :], aux_send.at[i], aux_recv.at[i], up, gy)
        for i, (src, dst) in enumerate([(east_in, east_low), (flag_east_in, flag_low), (mask_in, mask_low)])
    ]
    aux_down = [
        remote(mask_in.at[:, 0, :, first_row, :], mask_high.at[:, :, first_row, :], aux_send.at[3], aux_recv.at[3], down, gy)
    ]
    aux_right = [
        remote(src.at[:, :, wide - 1], dst, aux_send.at[4 + i], aux_recv.at[4 + i], gx, to_right)
        for i, (src, dst) in enumerate([(north_in, north_left), (flag_north_in, flag_left), (mask_in, mask_left)])
    ]
    aux_left = [remote(mask_in.at[:, :, 0], mask_right, aux_send.at[7], aux_recv.at[7], gx, to_left)]

    def up_copy(k):
        return remote(
            modes_in.at[:, k, high - 1, :, last, :], low.at[:, k, :, last, :], up_send.at[k], low_recv.at[k], up, gy
        )

    def up_relay(k):
        return remote(
            modes_in.at[:, k, high - 1, :, last, :], relay.at[k, :, :, first, :], up_send.at[k], relay_recv.at[k], down, gy
        )

    def down_copy(k):
        return remote(
            modes_in.at[:, k, 0, :, first, :], high_side.at[:, k, :, start, :], down_send.at[k], high_recv.at[k], down, gy
        )

    def down_relay(k):
        return remote(
            modes_in.at[:, k, 0, :, first, :], relay.at[k, :, :, first, :], down_send.at[k], relay_recv.at[k], up, gy
        )

    def pass_up(k):
        return remote(
            relay.at[k, :, :, first, :], low.at[:, k, :, last, :], pass_send.at[k], low_recv.at[k], up_two, gy
        )

    def pass_down(k):
        return remote(
            relay.at[k, :, :, first, :], high_side.at[:, k, :, start, :], pass_send.at[k], high_recv.at[k], down_two, gy
        )

    def right_copy(k):
        return remote(modes_in.at[:, k, :, wide - 1], left.at[:, k], right_send.at[k], left_recv.at[k], gx, to_right)

    def left_copy(k):
        return remote(modes_in.at[:, k, :, 0], right.at[:, k], left_send.at[k], right_recv.at[k], gx, to_left)

    mean_up = remote(
        mean_in.at[:, high - 1, :, last, :], ext_mean.at[0, :, :, last, :], mean_send.at[0], mean_recv.at[0], up, gy
    )
    mean_down = remote(
        mean_in.at[:, 0, :, first, :], ext_mean.at[0, :, :, end, :], mean_send.at[1], mean_recv.at[1], down, gy
    )
    mean_right = remote(mean_in.at[:, :, wide - 1], left_mean.at[0], mean_send.at[2], mean_recv.at[2], gx, to_right)
    mean_left = remote(mean_in.at[:, :, 0], right_mean.at[0], mean_send.at[3], mean_recv.at[3], gx, to_left)

    def turn(k):
        return lax.rem(k, half)

    def send_relayed(k, carry):
        @pl.when(turn(k) < up_turns)
        def _():
            up_relay(k).start()

        @pl.when(turn(k) < down_turns)
        def _():
            down_relay(k).start()

        return carry

    def send_x_level(k, carry):
        @pl.when(has_up & (turn(k) >= up_turns))
        def _():
            up_copy(k).start()

        @pl.when(has_down & (turn(k) >= down_turns))
        def _():
            down_copy(k).start()

        return carry

    def pass_level(k):
        @pl.when(turn(k) < pass_up_turns)
        def _():
            up_relay(k).wait_recv()
            pass_up(k).start()

        @pl.when(turn(k) < pass_down_turns)
        def _():
            down_relay(k).wait_recv()
            pass_down(k).start()

    pl.semaphore_wait(barrier, sum(there.astype(jnp.int32) for there, x, y in beside))

    @pl.when(has_up)
    def _():
        for copy in aux_up:
            copy.start()

    @pl.when(has_down)
    def _():
        for copy in aux_down:
            copy.start()

    lax.fori_loop(0, levels, send_relayed, 0)
    lax.fori_loop(0, levels, send_x_level, 0)

    @pl.when(has_right)
    def _():
        for copy in aux_right:
            copy.start()

    @pl.when(has_left)
    def _():
        for copy in aux_left:
            copy.start()

    def load_and_send(k, carry):
        for copy in load_level(k):
            copy.start()

        @pl.when(has_right)
        def _():
            right_copy(k).start()

        @pl.when(has_left)
        def _():
            left_copy(k).start()

        return carry

    for copy in plane_loads:
        copy.start()

    lax.fori_loop(0, levels, load_and_send, 0)
    nothing = jnp.zeros((count, SUB, LANES), jnp.float32)

    def zero_beyond(k, carry):
        for t in range(wide):
            ext[:, k, t, :SUB, :] = nothing
            ext[:, k, t, SUB + size_x :, :] = nothing
            low[:, k, t, SUB:, :] = nothing
            high_side[:, k, t, :SUB, :] = nothing
        return carry

    lax.fori_loop(0, levels, zero_beyond, 0)

    def zero_low(k, carry):
        for t in range(wide):
            low[:, k, t, :SUB, :] = nothing
            ext_mean[:, k, t, :SUB, :] = jnp.zeros((1, SUB, LANES), jnp.float32)
        return carry

    def zero_high(k, carry):
        for t in range(wide):
            high_side[:, k, t, SUB:, :] = nothing
            ext_mean[:, k, t, SUB + size_x :, :] = jnp.zeros((1, SUB, LANES), jnp.float32)
        return carry

    def zero_left(k, carry):
        left[:, k] = jnp.zeros((count, high, SUB, LANES), jnp.float32)
        left_mean[:, k] = jnp.zeros((1, high, SUB, LANES), jnp.float32)
        return carry

    def zero_right(k, carry):
        right[:, k] = jnp.zeros((count, high, SUB, LANES), jnp.float32)
        right_mean[:, k] = jnp.zeros((1, high, SUB, LANES), jnp.float32)
        return carry

    @pl.when(~has_down)
    def _():
        lax.fori_loop(0, levels, zero_low, 0)
        for ref in (east_low, flag_low, mask_low):
            ref[...] = jnp.zeros_like(ref)

    @pl.when(~has_up)
    def _():
        lax.fori_loop(0, levels, zero_high, 0)
        mask_high[...] = jnp.zeros_like(mask_high)

    @pl.when(~has_left)
    def _():
        lax.fori_loop(0, levels, zero_left, 0)
        for ref in (north_left, flag_left, mask_left):
            ref[...] = jnp.zeros_like(ref)

    @pl.when(~has_right)
    def _():
        lax.fori_loop(0, levels, zero_right, 0)
        mask_right[...] = jnp.zeros_like(mask_right)

    total[...] = jnp.zeros_like(total)

    for copy in plane_loads:
        copy.wait()

    for k in range(min(2, levels)):
        for copy in load_level(k):
            copy.wait()

    for k in range(min(AHEAD, levels)):
        pass_level(k)

    @pl.when(has_down)
    def _():
        for copy in aux_up:
            copy.wait_recv()

    @pl.when(has_up)
    def _():
        for copy in aux_down:
            copy.wait_recv()

    @pl.when(has_left)
    def _():
        for copy in aux_right:
            copy.wait_recv()

    @pl.when(has_right)
    def _():
        for copy in aux_left:
            copy.wait_recv()

    lane = lax.broadcasted_iota(jnp.int32, (SUB, LANES), 1)

    def plane(ref, k):
        return jnp.concatenate(
            [jnp.concatenate([f32(ref[k, h, t]) for t in range(wide)], axis=1) for h in range(high)], axis=0
        )

    def edge_row(ref, k, row):
        return jnp.concatenate([f32(ref[k, t, row : row + 1, :]) for t in range(wide)], axis=1)

    def edge_column(ref, k, column):
        return jnp.concatenate([f32(ref[k, h])[:, column : column + 1] for h in range(high)], axis=0)

    def level_coefs(k):
        wet = plane(mask, k)
        dx = stencil(
            plane(east, k), plane(flag_east, k), wet,
            edge_row(east_low, k, SUB - 1), edge_row(flag_low, k, SUB - 1), edge_row(mask_low, k, SUB - 1),
            edge_row(mask_high, k, 0), 0,
        )
        dy = stencil(
            plane(north, k), plane(flag_north, k), wet,
            edge_column(north_left, k, LANES - 1), edge_column(flag_left, k, LANES - 1),
            edge_column(mask_left, k, LANES - 1), edge_column(mask_right, k, 0), 1,
        )
        upright = vert_diff * wet
        return [dx[s] for s in SHIFTS] + [dy[s] for s in SHIFTS] + [dx[0] + dy[0] - 2.0 * upright, upright]

    def moved(row, s):
        if s < 0:
            mixed = jnp.where(lane >= LANES + s, row[0], row[1])
        else:
            mixed = jnp.where(lane < s, row[2], row[1])
        return pltpu.roll(mixed, (-s) % LANES, 1)

    def tendency(weights, f, k, h, t, cells, beside_left, beside_right):
        above = jnp.minimum(k + 1, levels - 1)
        below = jnp.maximum(k - 1, 0)
        base = SUB + SUB * h
        cut = slice(base, base + SUB)
        c = cells[f, k, t, cut, :]
        before = cells[f, k, t - 1, cut, :] if t > 0 else beside_left[f, k, h]
        after = cells[f, k, t + 1, cut, :] if t < wide - 1 else beside_right[f, k, h]
        row = [before, c, after]
        value = weights[12] * c + weights[13] * (cells[f, above, t, cut, :] + cells[f, below, t, cut, :])
        for i, s in enumerate(SHIFTS):
            value += weights[i] * cells[f, k, t, base + s : base + s + SUB, :]
            value += weights[6 + i] * moved(row, s)
        return value

    contract = (((1,), (1,)), ((), ()))
    def along_x(step):
        return [
            (gx + step < nx, jnp.minimum(gx + step, nx - 1), gy),
            (gx >= step, jnp.maximum(gx - step, 0), gy),
        ]

    def along_y(step):
        return [
            (gy + step < ny, gx, jnp.minimum(gy + step, ny - 1)),
            (gy >= step, gx, jnp.maximum(gy - step, 0)),
        ]

    rounds = [along_y(step) for step in doublings(1, ny)]
    rounds += [along_x(1) + along_x(2)] + [along_x(step) for step in doublings(2, nx)]

    def split(values):
        coarse = values.astype(jnp.bfloat16)
        return coarse, (values - f32(coarse)).astype(jnp.bfloat16)

    def inner_tendency(k):
        for i, value in enumerate(level_coefs(k)):
            coefs[k, i] = value

        @pl.when(has_left)
        def _():
            right_copy(k).wait_recv()

        @pl.when(has_right)
        def _():
            left_copy(k).wait_recv()

        for h in range(high):
            for t in range(wide):
                weights = [
                    coefs[k, i, SUB * h : SUB * (h + 1), LANES * t : LANES * (t + 1)] for i in range(len(SHIFTS) * 2 + 2)
                ]
                for f in range(count):
                    tend[k, h * wide + t, SUB * f : SUB * (f + 1), :] = tendency(
                        weights, f, k, h, t, ext, left, right
                    )

    def level(k, carry):
        @pl.when(k + AHEAD < levels)
        def _():
            pass_level(k + AHEAD)

        @pl.when(k == max(levels - 1, 0))
        def _():
            for there, copy in ((has_up, mean_up), (has_down, mean_down), (has_right, mean_right), (has_left, mean_left)):

                @pl.when(there)
                def _():
                    copy.start()

        for n in range(len(rounds) + 1):

            @pl.when(k == n * levels // (len(rounds) + 1))
            def _():
                if n > 0:
                    heard = sum(there.astype(jnp.int32) for there, x, y in rounds[n - 1])
                    pl.semaphore_wait(known.at[n - 1], heard)
                if n < len(rounds):
                    for there, x, y in rounds[n]:

                        @pl.when(there)
                        def _():
                            pl.semaphore_signal(known.at[n], inc=1, device_id=(x, y), device_id_type=MESH)

        @pl.when(k + 2 < levels)
        def _():
            for copy in load_level(k + 2):
                copy.wait()

        @pl.when(k + 1 < levels)
        def _():
            inner_tendency(k + 1)

        @pl.when(has_down)
        def _():
            up_copy(k).wait_recv()

        @pl.when(has_up)
        def _():
            down_copy(k).wait_recv()

        for h, side, taps in ((0, low, (0, 1, 2)), (high - 1, high_side, (3, 4, 5))):
            for t in range(wide):
                edge = [
                    coefs[k, i, SUB * h : SUB * (h + 1), LANES * t : LANES * (t + 1)] for i in range(len(SHIFTS))
                ]
                for f in range(count):
                    cut = slice(SUB * f, SUB * (f + 1))
                    value = tend[k, h * wide + t, cut, :]
                    for i in taps:
                        base = SHIFTS[i] + (SUB if i < HALO else 0)
                        value += edge[i] * side[f, k, t, base : base + SUB, :]
                    tend[k, h * wide + t, cut, :] = value
        u = jnp.concatenate(
            [
                ext[:, k, t, SUB + SUB * h : SUB + SUB * (h + 1), :].reshape(count * SUB, LANES)
                for h in range(high)
                for t in range(wide)
            ],
            axis=1,
        )
        v = jnp.concatenate([tend[k, i] for i in range(high * wide)], axis=1)
        coarse, fine = split(jnp.concatenate([u, v], axis=0))
        total[...] += lax.dot_general(
            jnp.concatenate([coarse, fine], axis=0), coarse, contract, preferred_element_type=jnp.float32
        )
        return carry

    inner_tendency(0)
    lax.fori_loop(0, levels, level, 0)

    others = [(i, j) for i in range(nx) for j in range(ny) if i or j]
    me = gx * ny + gy

    def other(step):
        return next_x(step[0]), next_y(step[1])

    def part_copy(n, slot):
        return remote(mine, slots.at[slot], part_send.at[n], part_recv.at[slot], *other(others[n]))

    two, tall = 2 * count, 2 * count * SUB

    def thirds(values, axis):
        coarse = values.astype(jnp.bfloat16)
        rest = values - f32(coarse)
        middling = rest.astype(jnp.bfloat16)
        return jnp.concatenate([coarse, middling, (rest - f32(middling)).astype(jnp.bfloat16)], axis=axis)

    def group(shape, axis):
        return lax.rem(lax.broadcasted_iota(jnp.int32, shape, axis), tall) // SUB

    kept = (lax.broadcasted_iota(jnp.int32, (tall, tall), 0) % SUB) == (
        lax.broadcasted_iota(jnp.int32, (tall, tall), 1) % SUB
    )
    pick = (
        group((two, 3 * tall), 1) == lax.broadcasted_iota(jnp.int32, (two, 3 * tall), 0)
    ).astype(jnp.bfloat16)
    spread = (
        group((3 * tall, two), 0) == lax.broadcasted_iota(jnp.int32, (3 * tall, two), 1)
    ).astype(jnp.bfloat16)
    picked = jnp.concatenate(
        [
            jnp.dot(pick, thirds(jnp.where(kept, part, 0.0), 0), preferred_element_type=jnp.float32)
            for part in (total[:tall, :], total[tall:, :])
        ],
        axis=0,
    )
    both = jnp.dot(thirds(picked, 1), spread, preferred_element_type=jnp.float32)
    cross = both[two:, :]
    summed = both[:two, :] + cross + cross.T
    row = lax.broadcasted_iota(jnp.int32, (count, count), 0)
    col = lax.broadcasted_iota(jnp.int32, (count, count), 1)
    outer = summed[count:, count:]
    kept = jnp.concatenate([jnp.where(col >= row, summed[:count, :count], outer), summed[count:, :count]], axis=1)
    height = gram.shape[0] - 1
    mine[:height, :] = jnp.concatenate([kept[height * b : height * (b + 1), :] for b in range(count // height)], axis=1)
    mine[height:, :] = jnp.concatenate(
        [
            jnp.sum(jnp.where(row == col, outer, 0.0), axis=0, keepdims=True),
            jnp.zeros((1, LANES - count), jnp.float32),
        ],
        axis=1,
    )
    slots[me] = mine[...]
    for n in range(len(others)):
        part_copy(n, me).start()

    @pl.when(has_down)
    def _():
        mean_up.wait_recv()

    @pl.when(has_up)
    def _():
        mean_down.wait_recv()

    @pl.when(has_left)
    def _():
        mean_right.wait_recv()

    @pl.when(has_right)
    def _():
        mean_left.wait_recv()

    def mean_level(k, carry):
        for h in range(high):
            for t in range(wide):
                weights = [
                    coefs[k, i, SUB * h : SUB * (h + 1), LANES * t : LANES * (t + 1)] for i in range(len(SHIFTS) * 2 + 2)
                ]
                value = tendency(weights, 0, k, h, t, ext_mean, left_mean, right_mean)
                mean_next[k, h, t] = ext_mean[0, k, t, SUB + SUB * h : SUB + SUB * (h + 1), :] + time_step * value
        return carry

    lax.fori_loop(0, levels, mean_level, 0)

    def settle(k, carry):
        @pl.when(has_up)
        def _():
            up_copy(k).wait_send()

        @pl.when(has_down)
        def _():
            down_copy(k).wait_send()

        @pl.when((turn(k) < pass_down_turns) | (turn(k) < pass_up_turns))
        def _():
            pass_down(k).wait_send()

        @pl.when(has_right)
        def _():
            right_copy(k).wait_send()

        @pl.when(has_left)
        def _():
            left_copy(k).wait_send()

        return carry

    lax.fori_loop(0, levels, settle, 0)
    for there, copies in (
        (has_up, aux_up + [mean_up]),
        (has_down, aux_down + [mean_down]),
        (has_right, aux_right + [mean_right]),
        (has_left, aux_left + [mean_left]),
    ):

        @pl.when(there)
        def _():
            for copy in copies:
                copy.wait_send()

    for n, step in enumerate(others):
        x, y = other(step)
        part_copy(n, x * ny + y).wait_recv()
    summed = slots[0]
    for n in range(1, nx * ny):
        summed = summed + slots[n]
    gram[...] = summed
    for n in range(len(others)):
        part_copy(n, me).wait_send()


def solve(packed, count, cells):
    two = 2 * count
    height = packed.shape[0] - 1
    kept = (
        jnp.concatenate([packed[:height, two * b : two * (b + 1)] for b in range(count // height)], axis=0) / cells
    )
    flipped = kept.T
    row = lax.broadcasted_iota(jnp.int32, (count, count), 0)
    col = lax.broadcasted_iota(jnp.int32, (count, count), 1)
    mixed, mirrored = kept[:, :count], flipped[:count, :]
    outer = jnp.where(row == col, packed[height:, :count] / cells, jnp.where(col < row, mixed, mirrored))
    total = jnp.concatenate(
        [
            jnp.concatenate([jnp.where(col >= row, mixed, mirrored), flipped[count:, :]], axis=1),
            jnp.concatenate([kept[:, count:], outer], axis=1),
        ],
        axis=0,
    )
    row = lax.broadcasted_iota(jnp.int32, (count, two), 0)
    col = lax.broadcasted_iota(jnp.int32, (count, two), 1)
    contract = (((1,), (1,)), ((), ()))
    update = jnp.where(
        col < count,
        jnp.where(col == row, 1.0, 0.0) - time_step * total[count:, :],
        jnp.where(col == row + count, time_step, 0.0),
    )
    padding = jnp.zeros((count, two), jnp.float32)
    halfway = jnp.dot(update, total, precision=HIGHEST, preferred_element_type=jnp.float32)
    work = lax.dot_general(
        halfway,
        jnp.concatenate([update, padding], axis=0),
        contract,
        precision=HIGHEST,
        preferred_element_type=jnp.float32,
    )
    work = work + jnp.where(col == row + count, 1.0, 0.0)
    for first in range(0, count, BLOCK):
        block = range(first, min(first + BLOCK, count))
        columns = {j: jnp.broadcast_to(work[:, j : j + 1], (count, two)) for j in block}
        for j in block:
            scale = lax.rsqrt(columns[j][j : j + 1, :])
            pivot_row = work[j : j + 1, :] * scale
            column = columns[j] * scale
            work = jnp.where(row > j, work - column * pivot_row, jnp.where(row == j, pivot_row, work))
            for m in block:
                if m > j:
                    columns[m] = columns[m] - column * column[m : m + 1, :]
    factor = jnp.where(col >= row, work, 0.0)[:, :count]
    inverse = jnp.where(col >= count, work, 0.0)
    mix = jnp.dot(
        inverse,
        jnp.concatenate([padding, update], axis=0),
        precision=HIGHEST,
        preferred_element_type=jnp.float32,
    )
    return factor, mix


def combine_kernel(cells, ext, tend, mean, packed, out, mean_out, factor, result, weights, mean_sem, out_sem):
    count, levels, wide, tall, _ = ext.shape
    high = tall // SUB - 2
    tall, both_tall = count * SUB, 2 * count * SUB

    def store(k):
        return pltpu.make_async_copy(result.at[:, k], out.at[:, k], out_sem.at[k])

    store_mean = pltpu.make_async_copy(mean, mean_out, mean_sem)
    store_mean.start()
    factor[...], mix = solve(packed[...], count, cells)
    coarse = mix.astype(jnp.bfloat16)
    halves = jnp.concatenate([f32(coarse), mix - f32(coarse)], axis=0).astype(jnp.bfloat16)
    spread = (
        lax.broadcasted_iota(jnp.int32, (both_tall, 2 * count), 0) // SUB
        == lax.broadcasted_iota(jnp.int32, (both_tall, 2 * count), 1)
    ).astype(jnp.bfloat16)
    along = (
        lax.broadcasted_iota(jnp.int32, (2 * count, both_tall), 1) // SUB
        == lax.broadcasted_iota(jnp.int32, (2 * count, both_tall), 0)
    ).astype(jnp.bfloat16)
    tall_halves = jnp.dot(spread, halves, preferred_element_type=jnp.float32).astype(jnp.bfloat16)
    whole = jnp.dot(tall_halves, along, preferred_element_type=jnp.float32)
    row = lax.broadcasted_iota(jnp.int32, (both_tall, both_tall), 0)
    col = lax.broadcasted_iota(jnp.int32, (both_tall, both_tall), 1)
    weights[...] = jnp.where((row % SUB) == (col % SUB), whole, 0.0).astype(jnp.bfloat16)

    def level(k, carry):
        both = jnp.concatenate(
            [
                jnp.concatenate(
                    [
                        ext[:, k, t, SUB + SUB * h : SUB + SUB * (h + 1), :].reshape(tall, LANES),
                        tend[k, h * wide + t],
                    ],
                    axis=0,
                )
                for h in range(high)
                for t in range(wide)
            ],
            axis=1,
        )
        coarse = both.astype(jnp.bfloat16)
        fine = (both - coarse.astype(jnp.float32)).astype(jnp.bfloat16)
        main = jnp.dot(weights[...], coarse, preferred_element_type=jnp.float32)
        mixed = main[:tall] + (main[tall:] + jnp.dot(weights[:tall, :], fine, preferred_element_type=jnp.float32))
        for h in range(high):
            for t in range(wide):
                i = h * wide + t
                result[:, k, h, t] = mixed[:, LANES * i : LANES * (i + 1)].reshape(count, SUB, LANES)
        store(k).start()
        return carry

    lax.fori_loop(0, levels, level, 0, unroll=8)

    def settle(k, carry):
        store(k).wait()
        return carry

    lax.fori_loop(0, levels, settle, 0)
    store_mean.wait()


def section(mean_field, mode_fields, velocity_east, velocity_north, flag_east, flag_north, ocean_mask):
    count, levels, size_x, size_y = mode_fields.shape
    nx, ny = lax.axis_size("gx"), lax.axis_size("gy")
    high, wide = size_x // SUB, size_y // LANES
    real, whole = jnp.float32, jnp.int32
    anywhere = pl.BlockSpec(memory_space=pl.ANY)
    vmem = pl.BlockSpec(memory_space=pltpu.VMEM)
    modes = blocked(mode_fields)
    planes = [blocked(a) for a in (mean_field, velocity_east, velocity_north, flag_east, flag_north, ocean_mask)]
    plane = (levels, high, wide, SUB, LANES)
    tall = 2 * count * SUB
    packed = (2 * count * count // LANES + 1, LANES)
    spots = len(SHIFTS) * 2 + 2
    dma = pltpu.SemaphoreType.DMA
    rounds = len(doublings(1, ny)) + 1 + len(doublings(2, nx))
    edge_row, edge_side = (levels, wide, SUB, LANES), (levels, high, SUB, LANES)
    ext, tend, mean_next, gram = pl.pallas_call(
        functools.partial(tend_kernel, nx, ny),
        in_specs=[pl.BlockSpec(memory_space=pltpu.HBM)] * 7,
        out_specs=[vmem] * 4,
        out_shape=[
            pltpu.VMEM((count, levels, wide, size_x + 2 * SUB, LANES), real),
            pltpu.VMEM((levels, high * wide, count * SUB, LANES), real),
            pltpu.VMEM(plane, real),
            pltpu.VMEM(packed, real),
        ],
        scratch_shapes=[
            pltpu.VMEM((count, levels, high, SUB, LANES), real),
            pltpu.VMEM((count, levels, high, SUB, LANES), real),
            pltpu.VMEM((1, levels, wide, size_x + 2 * SUB, LANES), real),
            pltpu.VMEM((1, levels, high, SUB, LANES), real),
            pltpu.VMEM((1, levels, high, SUB, LANES), real),
            pltpu.VMEM((levels, count, wide, SUB, LANES), real),
            pltpu.VMEM(plane, real),
            pltpu.VMEM(plane, real),
            pltpu.VMEM(plane, whole),
            pltpu.VMEM(plane, whole),
            pltpu.VMEM(plane, whole),
            pltpu.VMEM(edge_row, real),
            pltpu.VMEM(edge_row, whole),
            pltpu.VMEM(edge_row, whole),
            pltpu.VMEM(edge_row, whole),
            pltpu.VMEM(edge_side, real),
            pltpu.VMEM(edge_side, whole),
            pltpu.VMEM(edge_side, whole),
            pltpu.VMEM(edge_side, whole),
            pltpu.VMEM((levels, spots, size_x, size_y), real),
            pltpu.VMEM((2 * tall, tall), real),
            pltpu.VMEM((count, levels, wide, 2 * SUB, LANES), real),
            pltpu.VMEM((count, levels, wide, 2 * SUB, LANES), real),
            pltpu.VMEM(packed, real),
            pltpu.VMEM((nx * ny,) + packed, real),
            dma((levels, high)),
            dma((5 + high,)),
        ]
        + [dma((levels,))] * 10
        + [dma((8,)), dma((8,)), dma((4,)), dma((4,)), pltpu.SemaphoreType.REGULAR((rounds,)), dma((nx * ny - 1,)), dma((nx * ny,))],
        compiler_params=pltpu.CompilerParams(collective_id=0, has_side_effects=True, vmem_limit_bytes=32 << 20),
        cost_estimate=pl.CostEstimate(flops=60 * mode_fields.size, bytes_accessed=12 * mode_fields.size, transcendentals=0),
    )(*[pltpu.with_memory_space_constraint(a, pltpu.HBM) for a in (modes, *planes)])

    cell_count = float(levels * size_x * size_y * nx * ny)
    modes_next, mean_next, factor = pl.pallas_call(
        functools.partial(combine_kernel, cell_count),
        in_specs=[vmem] * 4,
        out_specs=[anywhere, anywhere, vmem],
        out_shape=[
            jax.ShapeDtypeStruct(modes.shape, real),
            jax.ShapeDtypeStruct(plane, real),
            jax.ShapeDtypeStruct((count, count), real),
        ],
        scratch_shapes=[
            pltpu.VMEM(modes.shape, real),
            pltpu.VMEM((tall, tall), jnp.bfloat16),
            dma,
            dma((levels,)),
        ],
        compiler_params=pltpu.CompilerParams(vmem_limit_bytes=12 << 20),
    )(ext, tend, mean_next, gram)
    return unblocked(mean_next), unblocked(modes_next), factor


def solution(mesh):
    grid = P(None, "gx", "gy")
    modes = P(None, None, "gx", "gy")
    return jax.shard_map(
        section,
        mesh=mesh,
        in_specs=(grid, modes, grid, grid, grid, grid, grid),
        out_specs=(grid, modes, P()),
        check_vma=False,
    )
```
